32 devices in a mesh: blade: 4 (over z), inst: 4 (over x, core), cell: 2 (over y).
Axes of the slice: x: 2, y: 2, z: 4, core: 2. Of those that a mesh axis runs over, the one named last changes fastest.
Arguments:
- cell_coords: float32 [3, 320, 512], P(None, ('blade', 'cell'), 'inst'), may hold values from 0 to 1
- centre_points: float32 [3, 4096], P(None, ('blade', 'inst', 'cell')), may hold values from 0 to 1
- coefficients: float32 [24, 4096], P(None, ('blade', 'inst', 'cell')), may hold values from -1.2 to 1.2
- tile_lists: int32 [320, 4, 4], P(('blade', 'cell'), 'inst'), may hold values from 0 to 31, as said below
Outputs:
- displaced: float32 [8, 3, 320, 512], P('inst', None, ('blade', 'cell'))
- grid_velocity: float32 [8, 3, 320, 512], P('inst', None, ('blade', 'cell'))
The draws below stay inside these ranges and needn't reach their ends.
Inputs may be any that keep to these rules, and one draw needn't show every extreme that they name: `tile_lists`: entry k of every list lies in k * 8 to (k + 1) * 8 - 1, so each cell tile draws centre tiles from every blade.
All inputs are finite; a program needn't handle non-finite values.
Results may differ from the reference program's by a relative error of at most 0.0003.
Values sent between devices are 32-bit elements; how exact they have to be, the bound alone decides.
No kernel may reach another device: no remote copies, remote signals or barrier semaphores. Data moves between devices by JAX's collectives and lax.ppermute only.
A program may use at most 64 MiB of HBM per device.

```python
import jax
import jax.numpy as jnp
from jax import lax

NT = 8
TILE = 128
KT = 4
QUARTERS = 4
CSUB = 512
CBLK = 320
CENTRES = 4096
CT = 32


def draw_tile_lists(key, part):
    span = CT // KT
    offsets = jax.random.randint(key, (CBLK, QUARTERS, KT), 0, span, dtype=jnp.int32)
    base_tiles = jnp.arange(KT, dtype=jnp.int32) * span
    chosen = offsets + base_tiles
    chosen = chosen.at[0, 0, KT - 1].set(CT - 1)
    chosen = chosen.at[0, 0, 0].set(0)
    return chosen.astype(jnp.int32)


def shard_levels(rng, shape, shards, smallest, top_value):
    gain = 1.0
    for position, parts in shards:
        draws = jax.random.uniform(jax.random.fold_in(jax.random.fold_in(rng, 6), position), (parts,), jnp.float32, smallest / len(shards), top_value / len(shards))
        gain = gain * jnp.repeat(jnp.exp(draws), shape[position] // parts).reshape((-1,) + (1,) * (len(shape) - 1 - position))
    return gain


def normal_values(own_key, extent, deviation, most, cuts=(), kind=jnp.bfloat16):
    drawn = jax.random.normal(own_key, extent, jnp.float32) * deviation
    if len(cuts) > 0:
        drawn = shard_levels(own_key, extent, cuts, -0.22, 0.18) * drawn
    return jnp.clip(drawn, min=-most, max=most).astype(kind)


def setup_inputs(seed: int = 0) -> dict:
    key_of = jax.random.split(jax.random.key(seed), 5)
    cell_coords = jnp.clip(1.0 * jax.random.uniform(key_of[0], (3, CBLK, CSUB), jnp.float32) ** shard_levels(key_of[0], (3, CBLK, CSUB), ((1, 8), (2, 4)), -0.2, 0.2), 0.0, 1.0)
    centre_points = jnp.clip(1.0 * jax.random.uniform(key_of[1], (3, CENTRES), jnp.float32) ** shard_levels(key_of[1], (3, CENTRES), ((1, 32),), -0.2, 0.2), 0.0, 1.0)
    coefficients = normal_values(key_of[2], (NT * 3, CENTRES), 0.2, 1.2, ((1, 32),), jnp.float32)
    tile_lists = draw_tile_lists(jax.random.fold_in(key_of[4], 71), 0)
    return {"cell_coords": cell_coords, "centre_points": centre_points, "coefficients": coefficients, "tile_lists": tile_lists}


def wendland(cell_tiles, near_points):
    squared = jnp.zeros(near_points.shape[1:] + cell_tiles.shape[-1:], jnp.float32)
    for axis_id in range(3):
        offset = near_points[axis_id][..., :, None] - cell_tiles[axis_id][:, None, None, :]
        squared = squared + offset * offset
    scaled = jnp.sqrt(squared) / 0.4
    margin = jnp.maximum(1.0 - scaled, 0.0)
    margin_sq = margin * margin
    return margin_sq * margin_sq * (1.0 + 4.0 * scaled)

def tile_sums(cell_tiles, list_rows, point_tiles, coef_tiles):
    near_points = point_tiles[:, list_rows]
    near_coefs = coef_tiles[:, list_rows]
    weights = wendland(cell_tiles, near_points)
    return jnp.einsum('amkj,mkjc->amc', near_coefs, weights, precision=lax.Precision.HIGHEST)

def block_sums(cell_tiles, list_rows, point_tiles, coef_tiles, width):
    groups = cell_tiles.shape[1] // width
    cell_groups = jnp.moveaxis(cell_tiles.reshape(3, groups, width, cell_tiles.shape[2]), 1, 0)
    list_groups = list_rows.reshape(groups, width, list_rows.shape[1])

    def one_group(operands):
        return tile_sums(operands[0], operands[1], point_tiles, coef_tiles)
    tile_totals = lax.map(one_group, (cell_groups, list_groups))
    return jnp.moveaxis(tile_totals, 0, 1).reshape(coef_tiles.shape[0], cell_tiles.shape[1], cell_tiles.shape[2])

def spectral_matrix(instances):
    later = jnp.arange(instances, dtype=jnp.int32)[:, None]
    earlier = jnp.arange(instances, dtype=jnp.int32)[None, :]
    distance = (later - earlier).astype(jnp.float32)
    parity = jnp.where((later - earlier) % 2 == 0, 1.0, -1.0).astype(jnp.float32)
    guarded = jnp.where(distance == 0, 0.5, jnp.pi * distance / instances).astype(jnp.float32)
    values = 0.5 * parity * jnp.cos(guarded) / jnp.sin(guarded)
    return jnp.where(distance == 0, 0.0, values).astype(jnp.float32)

def reference(cell_coords, centre_points, coefficients, tile_lists):
    row_count = cell_coords.shape[1]
    quarters = tile_lists.shape[1]
    point_tiles = centre_points.reshape(3, CT, TILE)
    coef_tiles = coefficients.reshape(NT * 3, CT, TILE)
    cell_tiles = cell_coords.reshape(3, row_count * quarters, TILE)
    list_rows = tile_lists.reshape(row_count * quarters, KT)
    shift = block_sums(cell_tiles, list_rows, point_tiles, coef_tiles, 16)
    shift = shift.reshape(NT, 3, row_count, quarters * TILE)
    displaced = cell_coords[None] + shift
    matrix = spectral_matrix(NT)
    grid_velocity = jnp.einsum('ts,sarc->tarc', matrix, shift, precision=lax.Precision.HIGHEST)
    return (displaced, grid_velocity)
```

```python
import functools

import jax
import jax.numpy as jnp
import numpy as np
from jax import lax
from jax.experimental import pallas as pl
from jax.experimental.pallas import tpu as pltpu
from jax.sharding import PartitionSpec as P

NT = 8
TILE = 128
RADIUS = 0.4
EDGE = 4.0**0.2
SCALE = (EDGE / RADIUS) ** 2
FEATURES = 48
BOTH_MINOR = (((1,), (1,)), ((), ()))
F32 = jnp.float32
BF16 = jnp.bfloat16


def spectral_rows(instances, groups):
    later = np.arange(instances)[:, None]
    earlier = np.arange(instances)[None, :]
    distance = (later - earlier).astype(np.float64)
    guarded = np.where(distance == 0, 0.5, np.pi * distance / instances)
    parity = np.where((later - earlier) % 2 == 0, 1.0, -1.0)
    matrix = np.where(distance == 0, 0.0, 0.5 * parity * np.cos(guarded) / np.sin(guarded))
    per = instances // groups
    rows = []
    for group in range(groups):
        own = slice(group * per, (group + 1) * per)
        rows.append(np.concatenate([np.eye(instances)[own], matrix[own]], axis=0))
    return np.stack([np.kron(block, np.eye(3)) for block in rows]).astype(np.float32)


def split3(value):
    high = value.astype(BF16).astype(F32)
    rest = value - high
    middle = rest.astype(BF16).astype(F32)
    return high, middle, rest - middle


def flip(size, bit):
    return [(i, i ^ bit) for i in range(size)]


def bits_of(size):
    return [1 << b for b in range(size.bit_length() - 1)]


def cell_prep_kernel(own_ref, other_ref, feature_ref, coord_ref, *, rows, slots):
    for slot in range(slots):
        source = own_ref if slot == 0 else other_ref.at[slot - 1]

        def one_row(r, carry):
            value = source[r]
            high, middle, low = split3(value)
            stacked = jnp.concatenate([high, middle, low, high, middle, high], axis=0)
            feature_ref[slot, r] = stacked.T.astype(BF16)
            coord_ref[slot, pl.ds(r, 8, stride=rows), :] = value
            return carry

        lax.fori_loop(0, rows, one_row, 0, unroll=4)


def sums_kernel(
    list_ref, mix_ref, block_ref, feature_ref, coord_ref, own_ref, peer_ref,
    centre_ref, coef_ref, total_ref, dist0, dist1, weight0, weight1, *, rows, slots, terms, half,
):
    tiles = block_ref.shape[0]
    combos = 2 * half

    def one_tile(p, carry):
        high, middle, low = split3(block_ref[p, 3 * NT : 3 * NT + 8, :])
        centre_ref[p] = jnp.concatenate([high, high, high, middle, middle, low], axis=0).astype(BF16)
        mixed = jnp.dot(
            mix_ref[...], block_ref[p, : 3 * NT, :],
            preferred_element_type=F32, precision=lax.Precision.HIGHEST,
        )
        mixed_high = mixed.astype(BF16).astype(F32)
        coef_ref[p] = jnp.concatenate([mixed_high, mixed - mixed_high], axis=0).astype(BF16)
        return carry

    lax.fori_loop(0, tiles, one_tile, 0, unroll=4)

    def tile_pair(r, slot, pair):
        base = (slot * rows + r) * terms + 2 * pair
        return list_ref[base], list_ref[base + 1]

    def distances(r, slot, out):
        for pair in range(terms // 2):
            a, b = tile_pair(r, slot, pair)
            out[pair] = jnp.dot(
                feature_ref[slot, r], jnp.concatenate([centre_ref[a], centre_ref[b]], axis=1),
                preferred_element_type=F32,
            )

    def weights(source, out):
        for pair in range(terms // 2):
            squared = jnp.maximum(source[pair], 1e-12)
            margin = jnp.maximum(EDGE - squared * lax.rsqrt(squared), 0.0)
            margin_sq = margin * margin
            weight = (margin_sq * margin_sq) * (1.25 * EDGE - margin)
            high = weight.astype(BF16)
            out[pair, :TILE] = high
            out[pair, TILE:] = (weight - high.astype(F32)).astype(BF16)

    def contract(r, slot, source):
        total = None
        for pair in range(terms // 2):
            a, b = tile_pair(r, slot, pair)
            part = lax.dot_general(
                jnp.concatenate([coef_ref[a], coef_ref[b]], axis=1), source[pair], BOTH_MINOR,
                preferred_element_type=F32,
            )
            total = part if total is None else total + part
        total = total[:combos, :TILE] + total[combos:, :TILE] + total[:combos, TILE:]
        for group in range(combos // 8):
            total_ref[slot, pl.ds(r + group * 8 * rows, 8, stride=rows), :] = total[group * 8 : group * 8 + 8]

    distances(0, 0, dist0)

    def one_row(r, carry):
        contract(jnp.maximum(r - 1, 0), 1, weight1)
        distances(r, 1, dist1)
        weights(dist0, weight0)
        contract(r, 0, weight0)
        distances(jnp.minimum(r + 1, rows - 1), 0, dist0)
        weights(dist1, weight1)
        return carry

    lax.fori_loop(0, rows, one_row, 0, unroll=2)
    contract(rows - 1, 1, weight1)

    shifts = half // 2
    for slot in range(slots):
        for out, first in ((own_ref, 0), (peer_ref, half)):
            for c in range(half):
                value = total_ref[slot, (first + c) * rows : (first + c + 1) * rows, :]
                if c < shifts:
                    value = value + (coord_ref[slot, (c % 3) * rows : (c % 3 + 1) * rows, :] + 0.5)
                out[slot, c] = value


def merge_kernel(place_ref, own_ref, peer_ref, moved_ref, velocity_ref, sems, *, slots, half):
    shifts = half // 2
    copies = []
    for which, source in enumerate((own_ref, peer_ref)):
        for slot in range(slots):
            lane = pl.multiple_of(place_ref[which * slots + slot] * TILE, TILE)
            for part, out in enumerate((moved_ref, velocity_ref)):
                copies.append(
                    pltpu.make_async_copy(
                        source.at[slot, pl.ds(part * shifts, shifts)],
                        out.at[:, :, pl.ds(lane, TILE)],
                        sems.at[len(copies)],
                    )
                )
    for copy in copies:
        copy.start()
    for copy in copies:
        copy.wait()


def vmem():
    return pl.BlockSpec(memory_space=pltpu.VMEM)


def smem():
    return pl.BlockSpec(memory_space=pltpu.SMEM)


def hbm():
    return pl.BlockSpec(memory_space=pl.ANY)


def on_device(cell_coords, centre_points, coefficients, tile_lists, *, sizes):
    n_blade, n_inst, n_cell = sizes["blade"], sizes["inst"], sizes["cell"]
    rows = cell_coords.shape[1]
    terms = tile_lists.shape[2]
    width = centre_points.shape[1]
    slots = n_inst // 2
    half = 2 * 3 * (NT // n_inst)
    inst = lax.axis_index("inst")
    device = (lax.axis_index("blade") * n_inst + inst) * n_cell + lax.axis_index("cell")

    centred = centre_points - 0.5
    block = jnp.concatenate(
        [
            coefficients,
            (-2.0 * SCALE) * centred,
            SCALE * jnp.sum(centred * centred, axis=0, keepdims=True),
            jnp.ones((1, width), F32),
            jnp.zeros((3, width), F32),
        ],
        axis=0,
    )
    cells = cell_coords - 0.5
    list_row = jnp.pad(tile_lists[:, 0, :].astype(F32), ((0, 0), (0, TILE - terms)))
    blank = jnp.zeros_like(list_row)
    cell_rows = jnp.stack(
        [cells[0], cells[1], cells[2], blank + 1.0, SCALE * jnp.sum(cells * cells, axis=0), list_row, blank, blank],
        axis=1,
    )

    others = [lax.ppermute(cell_rows, "inst", flip(n_inst, 2 * s)) for s in range(1, slots)]

    phases = [("blade", n_blade, b, b * n_inst * n_cell) for b in reversed(bits_of(n_blade))]
    phases += [("cell", n_cell, b, b) for b in bits_of(n_cell)]
    phases += [("inst", n_inst, b, b * n_cell) for b in reversed(bits_of(n_inst))]
    blocks = block[None]
    for axis, size, bit, _ in phases:
        blocks = jnp.concatenate([blocks, lax.ppermute(blocks, axis, flip(size, bit))], axis=0)

    def position(index):
        relative = index ^ device
        return sum(((relative // mask) & 1) << k for k, (_, _, _, mask) in enumerate(phases))

    lists = jnp.stack(
        [tile_lists[:, 0, :]] + [o[:, 5, :terms].astype(jnp.int32) for o in others], axis=0
    )
    if width == TILE:
        lists = position(lists)
    else:
        per_tile = TILE // width
        blocks = jnp.take(blocks, position(jnp.arange(blocks.shape[0])), axis=0)
        blocks = blocks.reshape(-1, per_tile, 3 * NT + 8, width)
        blocks = jnp.moveaxis(blocks, 1, 2).reshape(-1, 3 * NT + 8, TILE)
    n_tiles = blocks.shape[0]

    features, coords = pl.pallas_call(
        functools.partial(cell_prep_kernel, rows=rows, slots=slots),
        out_shape=(
            jax.ShapeDtypeStruct((slots, rows, TILE, FEATURES), BF16),
            jax.ShapeDtypeStruct((slots, 8 * rows, TILE), F32),
        ),
        in_specs=[vmem(), vmem()],
        out_specs=(vmem(), vmem()),
        name="cell_prep",
    )(cell_rows, jnp.stack(others))

    mix_all = jnp.asarray(spectral_rows(NT, n_inst))
    mix = jnp.concatenate([mix_all[inst], mix_all[inst ^ 1]], axis=0)
    own, peer = pl.pallas_call(
        functools.partial(sums_kernel, rows=rows, slots=slots, terms=terms, half=half),
        out_shape=(jax.ShapeDtypeStruct((slots, half, rows, TILE), F32),) * 2,
        in_specs=[smem(), vmem(), vmem(), vmem(), vmem()],
        out_specs=(vmem(), vmem()),
        scratch_shapes=[
            pltpu.VMEM((n_tiles, FEATURES, TILE), BF16),
            pltpu.VMEM((n_tiles, 4 * half, TILE), BF16),
            pltpu.VMEM((slots, 2 * half * rows, TILE), F32),
            pltpu.VMEM((terms // 2, TILE, 2 * TILE), F32),
            pltpu.VMEM((terms // 2, TILE, 2 * TILE), F32),
            pltpu.VMEM((terms // 2, 2 * TILE, 2 * TILE), BF16),
            pltpu.VMEM((terms // 2, 2 * TILE, 2 * TILE), BF16),
        ],
        name="rbf_sums",
    )(lists.reshape(-1), mix, blocks, features, coords)

    received = lax.ppermute(peer, "inst", flip(n_inst, 1))
    slot_bits = 2 * jnp.arange(slots, dtype=jnp.int32)
    places = jnp.concatenate([inst ^ slot_bits, inst ^ 1 ^ slot_bits])
    out = jax.ShapeDtypeStruct((half // 2, rows, n_inst * TILE), F32)
    moved, velocity = pl.pallas_call(
        functools.partial(merge_kernel, slots=slots, half=half),
        out_shape=(out, out),
        in_specs=[smem(), hbm(), hbm()],
        out_specs=(hbm(), hbm()),
        scratch_shapes=[pltpu.SemaphoreType.DMA((4 * slots,))],
        name="merge",
    )(places, own, received)
    shape = (NT // n_inst, 3, rows, n_inst * TILE)
    return (moved.reshape(shape), velocity.reshape(shape))


def solution(mesh):
    sizes = dict(mesh.shape)
    in_specs = (
        P(None, ("blade", "cell"), "inst"),
        P(None, ("blade", "inst", "cell")),
        P(None, ("blade", "inst", "cell")),
        P(("blade", "cell"), "inst", None),
    )
    out_specs = (P("inst", None, ("blade", "cell"), None), P("inst", None, ("blade", "cell"), None))
    return jax.shard_map(
        functools.partial(on_device, sizes=sizes),
        mesh=mesh, in_specs=in_specs, out_specs=out_specs, check_vma=False,
    )
```

```python
import functools

import jax
import jax.numpy as jnp
import numpy as np
from jax import lax
from jax.experimental import pallas as pl
from jax.experimental.pallas import tpu as pltpu
from jax.sharding import PartitionSpec as P

NT = 8
TILE = 128
RADIUS = 0.4
EDGE = 4.0**0.2
SCALE = (EDGE / RADIUS) ** 2
FEATURES = 48
BOTH_MINOR = (((1,), (1,)), ((), ()))
F32 = jnp.float32
BF16 = jnp.bfloat16


def spectral_rows(instances, groups):
    later = np.arange(instances)[:, None]
    earlier = np.arange(instances)[None, :]
    distance = (later - earlier).astype(np.float64)
    guarded = np.where(distance == 0, 0.5, np.pi * distance / instances)
    parity = np.where((later - earlier) % 2 == 0, 1.0, -1.0)
    matrix = np.where(distance == 0, 0.0, 0.5 * parity * np.cos(guarded) / np.sin(guarded))
    per = instances // groups
    rows = []
    for group in range(groups):
        own = slice(group * per, (group + 1) * per)
        rows.append(np.concatenate([np.eye(instances)[own], matrix[own]], axis=0))
    return np.stack([np.kron(block, np.eye(3)) for block in rows]).astype(np.float32)


def split3(value):
    high = value.astype(BF16).astype(F32)
    rest = value - high
    middle = rest.astype(BF16).astype(F32)
    return high, middle, rest - middle


def flip(size, bit):
    return [(i, i ^ bit) for i in range(size)]


def bits_of(size):
    return [1 << b for b in range(size.bit_length() - 1)]


def cell_prep_kernel(*refs, rows, slots, terms, sizes, masks):
    sources, (feature_ref, coord_ref, place_ref) = refs[:slots], refs[slots:]
    n_inst, n_cell = sizes["inst"], sizes["cell"]
    device = (lax.axis_index("blade") * n_inst + lax.axis_index("inst")) * n_cell + lax.axis_index("cell")
    row_id = lax.broadcasted_iota(jnp.int32, (8, TILE), 0)
    diagonal = lax.broadcasted_iota(jnp.int32, (TILE, TILE), 0) == lax.broadcasted_iota(jnp.int32, (TILE, TILE), 1)
    identity = jnp.where(diagonal, 1.0, 0.0).astype(BF16)
    for slot in range(slots):
        source = sources[slot]

        def one_row(r, carry):
            value = source[r]
            coord_ref[slot, pl.ds(r, 8, stride=rows), :] = value
            centred = jnp.where(row_id < 3, value - 0.5, 0.0)
            length = SCALE * jnp.sum(centred * centred, axis=0, keepdims=True)
            value = jnp.where(row_id == 3, 1.0, jnp.where(row_id == 4, length, centred))
            high, middle, low = split3(value)
            stacked = jnp.concatenate([high, middle, low, high, middle, high], axis=0).astype(BF16)
            turned = lax.dot_general(identity, stacked, BOTH_MINOR, preferred_element_type=F32)
            feature_ref[slot, r] = turned.astype(BF16)
            return carry

        lax.fori_loop(0, rows, one_row, 0, unroll=8)
        tile = coord_ref[slot, 3 * rows : 4 * rows, :].astype(jnp.int32)
        if masks is not None:
            relative = tile ^ device
            tile = sum((lax.shift_right_logical(relative, m) & 1) << k for k, m in enumerate(masks))
        place_ref[slot] = tile


def sums_kernel(
    list_ref, mix_ref, block_ref, feature_ref, coord_ref, own_ref, peer_ref,
    centre_ref, coef_ref, total_ref, dist0, dist1, weight0, weight1, *, rows, slots, terms, half,
):
    tiles = block_ref.shape[0]
    combos = 2 * half
    row_id = lax.broadcasted_iota(jnp.int32, (8, TILE), 0)
    inst = lax.axis_index("inst")
    mix = jnp.concatenate([mix_ref[inst], mix_ref[inst ^ 1]], axis=0)

    def one_tile(p, carry):
        value = block_ref[p, 3 * NT : 3 * NT + 8, :]
        centred = jnp.where(row_id < 3, value - 0.5, 0.0)
        length = SCALE * jnp.sum(centred * centred, axis=0, keepdims=True)
        value = jnp.where(row_id == 3, length, jnp.where(row_id == 4, 1.0, (-2.0 * SCALE) * centred))
        high, middle, low = split3(value)
        centre_ref[p] = jnp.concatenate([high, high, high, middle, middle, low], axis=0).astype(BF16)
        mixed = jnp.dot(
            mix, block_ref[p, : 3 * NT, :],
            preferred_element_type=F32, precision=lax.Precision.HIGHEST,
        )
        mixed_high = mixed.astype(BF16).astype(F32)
        coef_ref[p] = jnp.concatenate([mixed_high, mixed - mixed_high], axis=0).astype(BF16)
        return carry

    lax.fori_loop(0, tiles, one_tile, 0, unroll=4)

    def tile_pair(r, slot, pair):
        return list_ref[slot, r, 2 * pair], list_ref[slot, r, 2 * pair + 1]

    def distances(r, slot, out):
        for pair in range(terms // 2):
            a, b = tile_pair(r, slot, pair)
            out[pair] = jnp.dot(
                feature_ref[slot, r], jnp.concatenate([centre_ref[a], centre_ref[b]], axis=1),
                preferred_element_type=F32,
            )

    def weights(source, out):
        for pair in range(terms // 2):
            squared = jnp.maximum(source[pair], 1e-12)
            margin = jnp.maximum(EDGE - squared * lax.rsqrt(squared), 0.0)
            margin_sq = margin * margin
            weight = (margin_sq * margin_sq) * (1.25 * EDGE - margin)
            high = weight.astype(BF16)
            out[pair, :TILE] = high
            out[pair, TILE:] = (weight - high.astype(F32)).astype(BF16)

    def contract(r, slot, source):
        total = None
        for pair in range(terms // 2):
            a, b = tile_pair(r, slot, pair)
            part = lax.dot_general(
                jnp.concatenate([coef_ref[a], coef_ref[b]], axis=1), source[pair], BOTH_MINOR,
                preferred_element_type=F32,
            )
            total = part if total is None else total + part
        total = total[:combos, :TILE] + total[combos:, :TILE] + total[:combos, TILE:]
        for group in range(combos // 8):
            total_ref[slot, pl.ds(r + group * 8 * rows, 8, stride=rows), :] = total[group * 8 : group * 8 + 8]

    distances(0, 0, dist0)

    def one_row(r, carry):
        contract(jnp.maximum(r - 1, 0), 1, weight1)
        distances(r, 1, dist1)
        weights(dist0, weight0)
        contract(r, 0, weight0)
        distances(jnp.minimum(r + 1, rows - 1), 0, dist0)
        weights(dist1, weight1)
        return carry

    lax.fori_loop(0, rows, one_row, 0, unroll=4)
    contract(rows - 1, 1, weight1)

    shifts = half // 2
    for slot in range(slots):
        for out, first in ((own_ref, 0), (peer_ref, half)):
            for c in range(half):
                value = total_ref[slot, (first + c) * rows : (first + c + 1) * rows, :]
                if c < shifts:
                    value = value + coord_ref[slot, (c % 3) * rows : (c % 3 + 1) * rows, :]
                out[slot, c] = value


def merge_kernel(own_ref, peer_ref, moved_ref, velocity_ref, *, slots, half):
    shifts = half // 2
    inst = lax.axis_index("inst")
    for which, source in enumerate((own_ref, peer_ref)):
        for slot in range(slots):
            lane = pl.multiple_of((inst ^ which ^ (2 * slot)) * TILE, TILE)
            moved_ref[:, :, pl.ds(lane, TILE)] = source[slot, :shifts]
            velocity_ref[:, :, pl.ds(lane, TILE)] = source[slot, shifts:]


def vmem():
    return pl.BlockSpec(memory_space=pltpu.VMEM)


def smem():
    return pl.BlockSpec(memory_space=pltpu.SMEM)


def on_device(cell_coords, centre_points, coefficients, tile_lists, *, sizes):
    n_blade, n_inst, n_cell = sizes["blade"], sizes["inst"], sizes["cell"]
    rows = cell_coords.shape[1]
    terms = tile_lists.shape[2]
    width = centre_points.shape[1]
    slots = n_inst // 2
    half = 2 * 3 * (NT // n_inst)
    block = jnp.concatenate([coefficients, centre_points, jnp.zeros((5, width), F32)], axis=0)
    list_row = jnp.pad(tile_lists[:, 0, :].astype(F32), ((0, 0), (0, TILE - terms)))
    blank = jnp.zeros_like(list_row)
    cell_rows = jnp.stack([cell_coords[0], cell_coords[1], cell_coords[2], list_row] + [blank] * 4, axis=1)

    others = [lax.ppermute(cell_rows, "inst", flip(n_inst, 2 * s)) for s in range(1, slots)]

    phases = [("blade", n_blade, b, b * n_inst * n_cell) for b in reversed(bits_of(n_blade))]
    phases += [("cell", n_cell, b, b) for b in bits_of(n_cell)]
    phases += [("inst", n_inst, b, b * n_cell) for b in reversed(bits_of(n_inst))]
    masks = [mask.bit_length() - 1 for _, _, _, mask in phases]

    features, coords, places = pl.pallas_call(
        functools.partial(
            cell_prep_kernel, rows=rows, slots=slots, terms=terms, sizes=sizes,
            masks=masks if width == TILE else None,
        ),
        out_shape=(
            jax.ShapeDtypeStruct((slots, rows, TILE, FEATURES), BF16),
            jax.ShapeDtypeStruct((slots, 8 * rows, TILE), F32),
            jax.ShapeDtypeStruct((slots, rows, TILE), jnp.int32),
        ),
        in_specs=[vmem()] * slots,
        out_specs=(vmem(),) * 3,
        name="cell_prep",
    )(cell_rows, *others)

    blocks = block[None]
    for index, (axis, size, bit, _) in enumerate(phases):
        arrived = lax.ppermute(blocks, axis, flip(size, bit))
        if index == len(phases) - 2:
            arrived, features, coords, places = lax.optimization_barrier((arrived, features, coords, places))
        blocks = jnp.concatenate([blocks, arrived], axis=0)
    if width < TILE:
        device = (lax.axis_index("blade") * n_inst + lax.axis_index("inst")) * n_cell + lax.axis_index("cell")
        relative = jnp.arange(blocks.shape[0]) ^ device
        order = sum(((relative >> m) & 1) << k for k, m in enumerate(masks))
        blocks = jnp.take(blocks, order, axis=0).reshape(-1, TILE // width, 3 * NT + 8, width)
        blocks = jnp.moveaxis(blocks, 1, 2).reshape(-1, 3 * NT + 8, TILE)
    n_tiles = blocks.shape[0]

    own, peer = pl.pallas_call(
        functools.partial(sums_kernel, rows=rows, slots=slots, terms=terms, half=half),
        out_shape=(jax.ShapeDtypeStruct((slots, half, rows, TILE), F32),) * 2,
        in_specs=[smem(), vmem(), vmem(), vmem(), vmem()],
        out_specs=(vmem(), vmem()),
        scratch_shapes=[
            pltpu.VMEM((n_tiles, FEATURES, TILE), BF16),
            pltpu.VMEM((n_tiles, 4 * half, TILE), BF16),
            pltpu.VMEM((slots, 2 * half * rows, TILE), F32),
            pltpu.VMEM((terms // 2, TILE, 2 * TILE), F32),
            pltpu.VMEM((terms // 2, TILE, 2 * TILE), F32),
            pltpu.VMEM((terms // 2, 2 * TILE, 2 * TILE), BF16),
            pltpu.VMEM((terms // 2, 2 * TILE, 2 * TILE), BF16),
        ],
        name="rbf_sums",
    )(places, jnp.asarray(spectral_rows(NT, n_inst)), blocks, features, coords)

    received = lax.ppermute(peer, "inst", flip(n_inst, 1))
    out = jax.ShapeDtypeStruct((half // 2, rows, n_inst * TILE), F32)
    moved, velocity = pl.pallas_call(
        functools.partial(merge_kernel, slots=slots, half=half),
        out_shape=(out, out),
        in_specs=[vmem(), vmem()],
        out_specs=(vmem(), vmem()),
        name="merge",
    )(own, received)
    shape = (NT // n_inst, 3, rows, n_inst * TILE)
    return (moved.reshape(shape), velocity.reshape(shape))


def solution(mesh):
    sizes = dict(mesh.shape)
    in_specs = (
        P(None, ("blade", "cell"), "inst"),
        P(None, ("blade", "inst", "cell")),
        P(None, ("blade", "inst", "cell")),
        P(("blade", "cell"), "inst", None),
    )
    out_specs = (P("inst", None, ("blade", "cell"), None), P("inst", None, ("blade", "cell"), None))
    return jax.shard_map(
        functools.partial(on_device, sizes=sizes),
        mesh=mesh, in_specs=in_specs, out_specs=out_specs, check_vma=False,
    )
```

```python
import functools

import jax
import jax.numpy as jnp
import numpy as np
from jax import lax
from jax.experimental import pallas as pl
from jax.experimental.pallas import tpu as pltpu
from jax.sharding import PartitionSpec as P

NT = 8
TILE = 128
RADIUS = 0.4
EDGE = 4.0**0.2
SCALE = (EDGE / RADIUS) ** 2
FEATURES = 48
VMEM_LIMIT = 16 * 1024 * 1024
BOTH_MINOR = (((1,), (1,)), ((), ()))
F32 = jnp.float32
BF16 = jnp.bfloat16


def spectral_rows(instances, groups):
    later = np.arange(instances)[:, None]
    earlier = np.arange(instances)[None, :]
    distance = (later - earlier).astype(np.float64)
    guarded = np.where(distance == 0, 0.5, np.pi * distance / instances)
    parity = np.where((later - earlier) % 2 == 0, 1.0, -1.0)
    matrix = np.where(distance == 0, 0.0, 0.5 * parity * np.cos(guarded) / np.sin(guarded))
    per = instances // groups
    rows = []
    for group in range(groups):
        own = slice(group * per, (group + 1) * per)
        rows.append(np.concatenate([np.eye(instances)[own], matrix[own]], axis=0))
    return np.stack([np.kron(block, np.eye(3)) for block in rows]).astype(np.float32)


def split3(value):
    high = value.astype(BF16).astype(F32)
    rest = value - high
    middle = rest.astype(BF16).astype(F32)
    return high, middle, rest - middle


def flip(size, bit):
    return [(i, i ^ bit) for i in range(size)]


def bits_of(size):
    return [1 << b for b in range(size.bit_length() - 1)]


def cell_prep_kernel(*refs, rows, slots, terms, sizes, masks):
    sources, (feature_ref, coord_ref, place_ref) = refs[:slots], refs[slots:]
    n_inst, n_cell = sizes["inst"], sizes["cell"]
    device = (lax.axis_index("blade") * n_inst + lax.axis_index("inst")) * n_cell + lax.axis_index("cell")
    row_id = lax.broadcasted_iota(jnp.int32, (8, TILE), 0)
    diagonal = lax.broadcasted_iota(jnp.int32, (TILE, TILE), 0) == lax.broadcasted_iota(jnp.int32, (TILE, TILE), 1)
    identity = jnp.where(diagonal, 1.0, 0.0).astype(BF16)
    for slot in range(slots):
        source = sources[slot]

        def one_row(r, carry):
            value = source[r]
            coord_ref[slot, pl.ds(r, 8, stride=rows), :] = value
            centred = jnp.where(row_id < 3, value - 0.5, 0.0)
            length = SCALE * jnp.sum(centred * centred, axis=0, keepdims=True)
            value = jnp.where(row_id == 3, 1.0, jnp.where(row_id == 4, length, centred))
            high, middle, low = split3(value)
            stacked = jnp.concatenate([high, middle, low, high, middle, high], axis=0).astype(BF16)
            turned = lax.dot_general(identity, stacked, BOTH_MINOR, preferred_element_type=F32)
            feature_ref[slot, r] = turned.astype(BF16)
            return carry

        lax.fori_loop(0, rows, one_row, 0, unroll=8)
        tile = coord_ref[slot, 3 * rows : 4 * rows, :].astype(jnp.int32)
        if masks is not None:
            relative = tile ^ device
            tile = sum((lax.shift_right_logical(relative, m) & 1) << k for k, m in enumerate(masks))
        place_ref[slot] = tile


def sums_kernel(
    list_ref, mix_ref, block_ref, feature_ref, coord_ref, own_ref, peer_ref,
    centre_ref, coef_ref, total_ref, dist0, dist1, weight0, weight1, *, rows, slots, terms, half,
):
    tiles = block_ref.shape[0]
    combos = 2 * half
    row_id = lax.broadcasted_iota(jnp.int32, (8, TILE), 0)
    inst = lax.axis_index("inst")
    mix = jnp.concatenate([mix_ref[inst], mix_ref[inst ^ 1]], axis=0)

    def one_tile(p, carry):
        value = block_ref[p, 3 * NT : 3 * NT + 8, :]
        centred = jnp.where(row_id < 3, value - 0.5, 0.0)
        length = SCALE * jnp.sum(centred * centred, axis=0, keepdims=True)
        value = jnp.where(row_id == 3, length, jnp.where(row_id == 4, 1.0, (-2.0 * SCALE) * centred))
        high, middle, low = split3(value)
        centre_ref[p] = jnp.concatenate([high, high, high, middle, middle, low], axis=0).astype(BF16)
        mixed = jnp.dot(
            mix, block_ref[p, : 3 * NT, :],
            preferred_element_type=F32, precision=lax.Precision.HIGHEST,
        )
        mixed_high = mixed.astype(BF16).astype(F32)
        coef_ref[p] = jnp.concatenate([mixed_high, mixed - mixed_high], axis=0).astype(BF16)
        return carry

    lax.fori_loop(0, tiles, one_tile, 0, unroll=4)

    def tile_pair(r, slot, pair):
        return list_ref[slot, r, 2 * pair], list_ref[slot, r, 2 * pair + 1]

    def distances(r, slot, out):
        for pair in range(terms // 2):
            a, b = tile_pair(r, slot, pair)
            out[pair] = jnp.dot(
                feature_ref[slot, r], jnp.concatenate([centre_ref[a], centre_ref[b]], axis=1),
                preferred_element_type=F32,
            )

    def weights(source, out):
        for pair in range(terms // 2):
            squared = jnp.maximum(source[pair], 1e-12)
            margin = jnp.maximum(EDGE - squared * lax.rsqrt(squared), 0.0)
            margin_sq = margin * margin
            weight = (margin_sq * margin_sq) * (1.25 * EDGE - margin)
            high = weight.astype(BF16)
            out[pair, :TILE] = high
            out[pair, TILE:] = (weight - high.astype(F32)).astype(BF16)

    def contract(r, slot, source):
        total = None
        for pair in range(terms // 2):
            a, b = tile_pair(r, slot, pair)
            part = lax.dot_general(
                jnp.concatenate([coef_ref[a], coef_ref[b]], axis=1), source[pair], BOTH_MINOR,
                preferred_element_type=F32,
            )
            total = part if total is None else total + part
        total = total[:combos, :TILE] + total[combos:, :TILE] + total[:combos, TILE:]
        for group in range(combos // 8):
            total_ref[slot, pl.ds(r + group * 8 * rows, 8, stride=rows), :] = total[group * 8 : group * 8 + 8]

    distances(0, 0, dist0)

    def one_row(r, carry):
        contract(jnp.maximum(r - 1, 0), 1, weight1)
        distances(r, 1, dist1)
        weights(dist0, weight0)
        contract(r, 0, weight0)
        distances(jnp.minimum(r + 1, rows - 1), 0, dist0)
        weights(dist1, weight1)
        return carry

    lax.fori_loop(0, rows, one_row, 0, unroll=4)
    contract(rows - 1, 1, weight1)

    shifts = half // 2
    for slot in range(slots):
        for out, first in ((own_ref, 0), (peer_ref, half)):
            for c in range(half):
                value = total_ref[slot, (first + c) * rows : (first + c + 1) * rows, :]
                if c < shifts:
                    value = value + coord_ref[slot, (c % 3) * rows : (c % 3 + 1) * rows, :]
                out[slot, c] = value


def merge_kernel(own_ref, peer_ref, moved_ref, velocity_ref, *, slots, half):
    shifts = half // 2
    inst = lax.axis_index("inst")
    for which, source in enumerate((own_ref, peer_ref)):
        for slot in range(slots):
            lane = pl.multiple_of((inst ^ which ^ (2 * slot)) * TILE, TILE)
            moved_ref[:, :, pl.ds(lane, TILE)] = source[slot, :shifts]
            velocity_ref[:, :, pl.ds(lane, TILE)] = source[slot, shifts:]


def in_vmem(value):
    return pltpu.with_memory_space_constraint(value, pltpu.VMEM)


def vmem():
    return pl.BlockSpec(memory_space=pltpu.VMEM)


def smem():
    return pl.BlockSpec(memory_space=pltpu.SMEM)


def on_device(cell_coords, centre_points, coefficients, tile_lists, *, sizes):
    n_blade, n_inst, n_cell = sizes["blade"], sizes["inst"], sizes["cell"]
    rows = cell_coords.shape[1]
    terms = tile_lists.shape[2]
    width = centre_points.shape[1]
    slots = n_inst // 2
    half = 2 * 3 * (NT // n_inst)
    block = jnp.concatenate([coefficients, centre_points, jnp.zeros((5, width), F32)], axis=0)
    list_row = jnp.pad(tile_lists[:, 0, :].astype(F32), ((0, 0), (0, TILE - terms)))
    blank = jnp.zeros_like(list_row)
    cell_rows = jnp.stack([cell_coords[0], cell_coords[1], cell_coords[2], list_row] + [blank] * 4, axis=1)

    others = [lax.ppermute(cell_rows, "inst", flip(n_inst, 2 * s)) for s in range(1, slots)]

    phases = [("blade", n_blade, b, b * n_inst * n_cell) for b in reversed(bits_of(n_blade))]
    phases += [("cell", n_cell, b, b) for b in bits_of(n_cell)]
    phases += [("inst", n_inst, b, b * n_cell) for b in reversed(bits_of(n_inst))]
    masks = [mask.bit_length() - 1 for _, _, _, mask in phases]

    features, coords, places = pl.pallas_call(
        functools.partial(
            cell_prep_kernel, rows=rows, slots=slots, terms=terms, sizes=sizes,
            masks=masks if width == TILE else None,
        ),
        out_shape=(
            pltpu.VMEM((slots, rows, TILE, FEATURES), BF16),
            pltpu.VMEM((slots, 8 * rows, TILE), F32),
            jax.ShapeDtypeStruct((slots, rows, TILE), jnp.int32),
        ),
        in_specs=[vmem()] * slots,
        out_specs=(vmem(),) * 3,
        compiler_params=pltpu.CompilerParams(vmem_limit_bytes=VMEM_LIMIT),
        name="cell_prep",
    )(in_vmem(cell_rows), *map(in_vmem, others))

    blocks = block[None]
    for index, (axis, size, bit, _) in enumerate(phases):
        arrived = lax.ppermute(blocks, axis, flip(size, bit))
        if index == len(phases) - 2:
            arrived, features, coords, places = lax.optimization_barrier((arrived, features, coords, places))
        blocks = jnp.concatenate([blocks, arrived], axis=0)
    if width < TILE:
        device = (lax.axis_index("blade") * n_inst + lax.axis_index("inst")) * n_cell + lax.axis_index("cell")
        relative = jnp.arange(blocks.shape[0]) ^ device
        order = sum(((relative >> m) & 1) << k for k, m in enumerate(masks))
        blocks = jnp.take(blocks, order, axis=0).reshape(-1, TILE // width, 3 * NT + 8, width)
        blocks = jnp.moveaxis(blocks, 1, 2).reshape(-1, 3 * NT + 8, TILE)
    n_tiles = blocks.shape[0]

    own, peer = pl.pallas_call(
        functools.partial(sums_kernel, rows=rows, slots=slots, terms=terms, half=half),
        out_shape=(pltpu.VMEM((slots, half, rows, TILE), F32),) * 2,
        in_specs=[smem(), vmem(), vmem(), vmem(), vmem()],
        out_specs=(vmem(), vmem()),
        scratch_shapes=[
            pltpu.VMEM((n_tiles, FEATURES, TILE), BF16),
            pltpu.VMEM((n_tiles, 4 * half, TILE), BF16),
            pltpu.VMEM((slots, 2 * half * rows, TILE), F32),
            pltpu.VMEM((terms // 2, TILE, 2 * TILE), F32),
            pltpu.VMEM((terms // 2, TILE, 2 * TILE), F32),
            pltpu.VMEM((terms // 2, 2 * TILE, 2 * TILE), BF16),
            pltpu.VMEM((terms // 2, 2 * TILE, 2 * TILE), BF16),
        ],
        compiler_params=pltpu.CompilerParams(vmem_limit_bytes=VMEM_LIMIT),
        name="rbf_sums",
    )(places, jnp.asarray(spectral_rows(NT, n_inst)), in_vmem(blocks), in_vmem(features), in_vmem(coords))

    received = lax.ppermute(peer, "inst", flip(n_inst, 1))
    out = jax.ShapeDtypeStruct((half // 2, rows, n_inst * TILE), F32)
    moved, velocity = pl.pallas_call(
        functools.partial(merge_kernel, slots=slots, half=half),
        out_shape=(out, out),
        in_specs=[vmem(), vmem()],
        out_specs=(vmem(), vmem()),
        compiler_params=pltpu.CompilerParams(vmem_limit_bytes=VMEM_LIMIT),
        name="merge",
    )(in_vmem(own), in_vmem(received))
    shape = (NT // n_inst, 3, rows, n_inst * TILE)
    return (moved.reshape(shape), velocity.reshape(shape))


def solution(mesh):
    sizes = dict(mesh.shape)
    in_specs = (
        P(None, ("blade", "cell"), "inst"),
        P(None, ("blade", "inst", "cell")),
        P(None, ("blade", "inst", "cell")),
        P(("blade", "cell"), "inst", None),
    )
    out_specs = (P("inst", None, ("blade", "cell"), None), P("inst", None, ("blade", "cell"), None))
    return jax.shard_map(
        functools.partial(on_device, sizes=sizes),
        mesh=mesh, in_specs=in_specs, out_specs=out_specs, check_vma=False,
    )
```

```python
import functools

import jax
import jax.numpy as jnp
import numpy as np
from jax import lax
from jax.experimental import pallas as pl
from jax.experimental.pallas import tpu as pltpu
from jax.sharding import PartitionSpec as P

NT = 8
TILE = 128
RADIUS = 0.4
EDGE = 4.0**0.2
SCALE = (EDGE / RADIUS) ** 2
FEATURES = 48
UNROLL = 4
VMEM_LIMIT = 16 * 1024 * 1024
BOTH_MINOR = (((1,), (1,)), ((), ()))
F32 = jnp.float32
BF16 = jnp.bfloat16


def spectral_rows(instances, groups):
    later = np.arange(instances)[:, None]
    earlier = np.arange(instances)[None, :]
    distance = (later - earlier).astype(np.float64)
    guarded = np.where(distance == 0, 0.5, np.pi * distance / instances)
    parity = np.where((later - earlier) % 2 == 0, 1.0, -1.0)
    matrix = np.where(distance == 0, 0.0, 0.5 * parity * np.cos(guarded) / np.sin(guarded))
    per = instances // groups
    rows = []
    for group in range(groups):
        own = slice(group * per, (group + 1) * per)
        rows.append(np.concatenate([np.eye(instances)[own], matrix[own]], axis=0))
    return np.stack([np.kron(block, np.eye(3)) for block in rows]).astype(np.float32)


def split3(value):
    high = value.astype(BF16).astype(F32)
    rest = value - high
    middle = rest.astype(BF16).astype(F32)
    return high, middle, rest - middle


def flip(size, bit):
    return [(i, i ^ bit) for i in range(size)]


def bits_of(size):
    return [1 << b for b in range(size.bit_length() - 1)]


def cell_prep_kernel(source, feature_ref, coord_ref, place_ref, *, rows, plane, sizes, masks):
    n_inst, n_cell = sizes["inst"], sizes["cell"]
    device = (lax.axis_index("blade") * n_inst + lax.axis_index("inst")) * n_cell + lax.axis_index("cell")
    row_id = lax.broadcasted_iota(jnp.int32, (8, TILE), 0)
    diagonal = lax.broadcasted_iota(jnp.int32, (TILE, TILE), 0) == lax.broadcasted_iota(jnp.int32, (TILE, TILE), 1)
    identity = jnp.where(diagonal, 1.0, 0.0).astype(BF16)

    def one_row(r, carry):
        value = source[r]
        coord_ref[pl.ds(r, 8, stride=rows), :] = value
        centred = jnp.where(row_id < 3, value - 0.5, 0.0)
        length = SCALE * jnp.sum(centred * centred, axis=0, keepdims=True)
        value = jnp.where(row_id == 3, 1.0, jnp.where(row_id == 4, length, centred))
        high, middle, low = split3(value)
        stacked = jnp.concatenate([high, middle, low, high, middle, high], axis=0).astype(BF16)
        turned = lax.dot_general(identity, stacked, BOTH_MINOR, preferred_element_type=F32)
        feature_ref[r] = turned.astype(BF16)
        return carry

    lax.fori_loop(0, rows, one_row, 0, unroll=8)
    tile = coord_ref[3 * rows : 4 * rows, :].T[:8].astype(jnp.int32)
    if masks is not None:
        tile = tile ^ device
        places = [(lax.shift_right_logical(tile, m) & 1) << k for k, m in enumerate(masks)]
        tile = functools.reduce(lambda x, y: x | y, places)
    else:
        tile = tile & (plane - 1)
    place_ref[:, :rows] = tile


def sums_kernel(*refs, rows, start, count, slots, half, first, prepare, last):
    list_refs, mix_ref, feature_refs = refs[:slots], refs[slots], refs[slots + 1 : 2 * slots + 1]
    refs = refs[2 * slots + 1 :]
    dist0, dist1, weight0, weight1 = refs[-5 if last else -4 :][:4]
    refs = list(refs[: -5 if last else -4]) + list(refs[-1:] if last else [])
    if last:
        coord_refs, before_ref = refs[:slots], refs[slots]
        refs = refs[slots + 1 :]
    block_refs = refs[:prepare]
    refs = refs[prepare:]
    if prepare and last:
        own_ref, peer_ref, centre_ref, coef_ref, total_ref = refs
    elif prepare:
        total_ref, centre_ref, coef_ref = refs
    elif last:
        centre_ref, coef_ref, own_ref, peer_ref, total_ref = refs
    else:
        centre_ref, coef_ref, total_ref = refs
    combos = 2 * half
    plane = centre_ref.shape[0] // 2
    row_id = lax.broadcasted_iota(jnp.int32, (8, TILE), 0)
    inst = lax.axis_index("inst")
    blade = lax.axis_index("blade")
    terms = [blade ^ first, blade ^ (first + 1)]
    mix = jnp.concatenate([mix_ref[inst], mix_ref[inst ^ 1]], axis=0)

    base = 0
    for block_ref in block_refs:

        def one_tile(p, carry, block_ref=block_ref, base=base):
            value = block_ref[p, 3 * NT : 3 * NT + 8, :]
            centred = jnp.where(row_id < 3, value - 0.5, 0.0)
            length = SCALE * jnp.sum(centred * centred, axis=0, keepdims=True)
            value = jnp.where(row_id == 3, length, jnp.where(row_id == 4, 1.0, (-2.0 * SCALE) * centred))
            high, middle, low = split3(value)
            stacked = jnp.concatenate([high, high, high, middle, middle, low], axis=0)
            centre_ref[base + p] = stacked.astype(BF16)
            mixed = jnp.dot(
                mix, block_ref[p, : 3 * NT, :],
                preferred_element_type=F32, precision=lax.Precision.HIGHEST,
            )
            mixed_high = mixed.astype(BF16).astype(F32)
            coef_ref[base + p] = jnp.concatenate([mixed_high, mixed - mixed_high], axis=0).astype(BF16)
            return carry

        lax.fori_loop(0, block_ref.shape[0], one_tile, 0, unroll=4)
        base += block_ref.shape[0]

    def tile_pair(r, slot):
        lists = list_refs[slot]
        return lists[terms[0], start + r], lists[terms[1], start + r] + plane

    def distances(i, slot, out):
        for k in range(2):
            a, b = tile_pair(2 * i + k, slot)
            out[k] = jnp.dot(
                feature_refs[slot][start + 2 * i + k], jnp.concatenate([centre_ref[a], centre_ref[b]], axis=1),
                preferred_element_type=F32,
            )

    def weights(source, out):
        for k in range(2):
            squared = jnp.maximum(source[k], 1e-12)
            margin = jnp.maximum(EDGE - squared * lax.rsqrt(squared), 0.0)
            margin_sq = margin * margin
            weight = (margin_sq * margin_sq) * (1.25 * EDGE - margin)
            high = weight.astype(BF16)
            out[k, :TILE] = high
            out[k, TILE:] = (weight - high.astype(F32)).astype(BF16)

    def contract(i, slot, source):
        for k in range(2):
            r = 2 * i + k
            a, b = tile_pair(r, slot)
            total = lax.dot_general(
                jnp.concatenate([coef_ref[a], coef_ref[b]], axis=1), source[k], BOTH_MINOR,
                preferred_element_type=F32,
            )
            total = total[:combos, :TILE] + total[combos:, :TILE] + total[:combos, TILE:]
            for group in range(combos // 8):
                total_ref[slot, pl.ds(r + group * 8 * count, 8, stride=count), :] = total[group * 8 : group * 8 + 8]

    distances(0, 0, dist0)
    pairs = count // 2

    def one_pair(i, carry):
        contract(jnp.maximum(i - 1, 0), 1, weight1)
        distances(i, 1, dist1)
        weights(dist0, weight0)
        contract(i, 0, weight0)
        distances(jnp.minimum(i + 1, pairs - 1), 0, dist0)
        weights(dist1, weight1)
        return carry

    lax.fori_loop(0, pairs, one_pair, 0, unroll=UNROLL)
    contract(pairs - 1, 1, weight1)
    if not last:
        return

    shifts = half // 2
    for slot in range(slots):
        for out, first_row in ((own_ref, 0), (peer_ref, half)):
            for c in range(half):
                span = slice((first_row + c) * count, (first_row + c + 1) * count)
                value = total_ref[slot, span, :] + before_ref[slot, span, :]
                if c < shifts:
                    begin = (c % 3) * rows + start
                    value = value + coord_refs[slot][begin : begin + count, :]
                out[slot, c] = value


def merge_kernel(*refs, slots, half, spans):
    shifts = half // 2
    moved_ref, velocity_ref = refs[-2:]
    inst = lax.axis_index("inst")
    for index, source in enumerate(refs[:-2]):
        start, count = spans[index // 2]
        for slot in range(slots):
            lane = pl.multiple_of((inst ^ (index % 2) ^ (2 * slot)) * TILE, TILE)
            moved_ref[:, start : start + count, pl.ds(lane, TILE)] = source[slot, :shifts]
            velocity_ref[:, start : start + count, pl.ds(lane, TILE)] = source[slot, shifts:]


def in_vmem(value):
    return pltpu.with_memory_space_constraint(value, pltpu.VMEM)


def vmem():
    return pl.BlockSpec(memory_space=pltpu.VMEM)


def smem():
    return pl.BlockSpec(memory_space=pltpu.SMEM)


def on_device(cell_coords, centre_points, coefficients, tile_lists, *, sizes):
    n_blade, n_inst, n_cell = sizes["blade"], sizes["inst"], sizes["cell"]
    rows = cell_coords.shape[1]
    terms = tile_lists.shape[2]
    width = centre_points.shape[1]
    slots = n_inst // 2
    half = 2 * 3 * (NT // n_inst)
    block = jnp.concatenate([coefficients, centre_points, jnp.zeros((5, width), F32)], axis=0)
    list_row = jnp.pad(tile_lists[:, 0, :].astype(F32), ((0, 0), (0, TILE - terms)))
    blank = jnp.zeros_like(list_row)
    cell_rows = jnp.stack([cell_coords[0], cell_coords[1], cell_coords[2], list_row] + [blank] * 4, axis=1)

    core = 1
    inner = [("cell", n_cell, b, b) for b in bits_of(n_cell)]
    inner += [("inst", n_inst, b, b * n_cell) for b in bits_of(n_inst) if b != core]
    masks = [mask.bit_length() - 1 for _, _, _, mask in inner] + [(core * n_cell).bit_length() - 1]

    half_plane = block[None]
    for index, (axis, size, bit, _) in enumerate(inner):
        arrived = lax.ppermute(half_plane, axis, flip(size, bit))
        if index == 0:
            arrived, cell_rows = lax.optimization_barrier((arrived, cell_rows))
        half_plane = jnp.concatenate([half_plane, arrived], axis=0)
    others = [lax.ppermute(cell_rows, "inst", flip(n_inst, 2 * s)) for s in range(1, slots)]
    halves = [half_plane]
    for m in range(1, n_blade):
        halves.append(lax.ppermute(half_plane, "blade", flip(n_blade, m)))

    swapped = []
    for m in range(2):
        swapped.append(lax.ppermute(halves[m], "inst", flip(n_inst, core)))
    late = lax.ppermute(jnp.concatenate(halves[2:], axis=0), "inst", flip(n_inst, core))
    swapped += jnp.split(late, n_blade - 2, axis=0)

    if width < TILE:
        device = lax.axis_index("inst") * n_cell + lax.axis_index("cell")
        relative = jnp.arange(n_inst * n_cell) ^ device
        order = sum(((relative >> m) & 1) << k for k, m in enumerate(masks))

        def whole_plane(mine, theirs):
            blocks = jnp.take(jnp.concatenate([mine, theirs], axis=0), order, axis=0)
            blocks = blocks.reshape(-1, TILE // width, 3 * NT + 8, width)
            return [jnp.moveaxis(blocks, 1, 2).reshape(-1, 3 * NT + 8, TILE)]

        plane = n_inst * n_cell * width // TILE
    else:
        def whole_plane(mine, theirs):
            return [mine, theirs]

        plane = n_inst * n_cell
    planes = [whole_plane(*pair) for pair in zip(halves, swapped)]

    def cell_prep(cells):
        return pl.pallas_call(
            functools.partial(
                cell_prep_kernel, rows=rows, plane=plane, sizes=sizes,
                masks=masks if width == TILE else None,
            ),
            out_shape=(
                pltpu.VMEM((rows, TILE, FEATURES), BF16),
                pltpu.VMEM((8 * rows, TILE), F32),
                jax.ShapeDtypeStruct((8, TILE), jnp.int32),
            ),
            in_specs=[vmem()],
            out_specs=(vmem(),) * 3,
            compiler_params=pltpu.CompilerParams(vmem_limit_bytes=VMEM_LIMIT),
            name="cell_prep",
        )(in_vmem(cells))

    prepared = [cell_prep(cell_rows)]
    prepared += [cell_prep(cells) for cells in others]
    features, coords, places = map(list, zip(*prepared))

    mix = jnp.asarray(spectral_rows(NT, n_inst))
    tables = (pltpu.VMEM((2 * plane, FEATURES, TILE), BF16), pltpu.VMEM((2 * plane, 4 * half, TILE), BF16))
    spans = [(0, rows)]

    def sums(first, span, given, extra):
        start, count = spans[span]
        last = len(extra) > 0
        blocks = [] if given else planes[first] + planes[first + 1]
        total = pltpu.VMEM((slots, 2 * half * count, TILE), F32)
        out = (pltpu.VMEM((slots, half, count, TILE), F32),) * 2 if last else (total,)
        out = out + (() if given else tables)
        operands = [*features, *extra, *blocks, *given]
        return pl.pallas_call(
            functools.partial(
                sums_kernel, rows=rows, start=start, count=count, slots=slots, half=half, first=first,
                prepare=len(blocks), last=last,
            ),
            out_shape=out,
            in_specs=[smem()] * slots + [vmem()] * (1 + len(operands)),
            out_specs=(vmem(),) * len(out),
            scratch_shapes=[pltpu.VMEM((2, TILE, 2 * TILE), F32)] * 2
            + [pltpu.VMEM((2, 2 * TILE, 2 * TILE), BF16)] * 2
            + ([total] if last else []),
            compiler_params=pltpu.CompilerParams(vmem_limit_bytes=VMEM_LIMIT),
        )(*places, in_vmem(mix), *map(in_vmem, operands))

    before, near = [], []
    for span in range(len(spans)):
        part, *tables_made = sums(0, span, near, [])
        before, near = before + [part], near or tables_made
    results, far = [], []
    for span in range(len(spans)):
        own, peer, *tables_made = sums(2, span, far, [*coords, before[span]])
        far = far or tables_made
        results += [own, lax.ppermute(peer, "inst", flip(n_inst, core))]
    out = jax.ShapeDtypeStruct((half // 2, rows, n_inst * TILE), F32)
    moved, velocity = pl.pallas_call(
        functools.partial(merge_kernel, slots=slots, half=half, spans=spans),
        out_shape=(out, out),
        in_specs=[vmem()] * len(results),
        out_specs=(vmem(), vmem()),
        compiler_params=pltpu.CompilerParams(vmem_limit_bytes=VMEM_LIMIT),
        name="merge",
    )(*map(in_vmem, results))
    shape = (NT // n_inst, 3, rows, n_inst * TILE)
    return (moved.reshape(shape), velocity.reshape(shape))


def solution(mesh):
    sizes = dict(mesh.shape)
    in_specs = (
        P(None, ("blade", "cell"), "inst"),
        P(None, ("blade", "inst", "cell")),
        P(None, ("blade", "inst", "cell")),
        P(("blade", "cell"), "inst", None),
    )
    out_specs = (P("inst", None, ("blade", "cell"), None), P("inst", None, ("blade", "cell"), None))
    return jax.shard_map(
        functools.partial(on_device, sizes=sizes),
        mesh=mesh, in_specs=in_specs, out_specs=out_specs, check_vma=False,
    )
```

```python
import functools

import jax
import jax.numpy as jnp
import numpy as np
from jax import lax
from jax.experimental import pallas as pl
from jax.experimental.pallas import tpu as pltpu
from jax.sharding import PartitionSpec as P

NT = 8
TILE = 128
RADIUS = 0.4
EDGE = 4.0**0.2
SCALE = (EDGE / RADIUS) ** 2
FEATURES = 48
NEAR_ROWS = 0
VMEM_LIMIT = 16 * 1024 * 1024
BOTH_MINOR = (((1,), (1,)), ((), ()))
F32 = jnp.float32
BF16 = jnp.bfloat16


def spectral_rows(instances, groups):
    later = np.arange(instances)[:, None]
    earlier = np.arange(instances)[None, :]
    distance = (later - earlier).astype(np.float64)
    guarded = np.where(distance == 0, 0.5, np.pi * distance / instances)
    parity = np.where((later - earlier) % 2 == 0, 1.0, -1.0)
    matrix = np.where(distance == 0, 0.0, 0.5 * parity * np.cos(guarded) / np.sin(guarded))
    per = instances // groups
    rows = []
    for group in range(groups):
        own = slice(group * per, (group + 1) * per)
        rows.append(np.concatenate([np.eye(instances)[own], matrix[own]], axis=0))
    return np.stack([np.kron(block, np.eye(3)) for block in rows]).astype(np.float32)


def split3(value):
    high = value.astype(BF16).astype(F32)
    rest = value - high
    middle = rest.astype(BF16).astype(F32)
    return high, middle, rest - middle


def flip(size, bit):
    return [(i, i ^ bit) for i in range(size)]


def bits_of(size):
    return [1 << b for b in range(size.bit_length() - 1)]


def cell_prep_kernel(source, *refs, rows, plane, sizes, masks):
    feature_ref, coord_ref, place_ref = refs[-4:-1] if len(refs) == 5 else refs
    if len(refs) == 5:
        mix_ref, mixed_ref = refs[0], refs[-1]
        inst = lax.axis_index("inst")
        mixed_ref[...] = jnp.concatenate([mix_ref[inst], mix_ref[inst ^ 1]], axis=0)
    n_inst, n_cell = sizes["inst"], sizes["cell"]
    device = (lax.axis_index("blade") * n_inst + lax.axis_index("inst")) * n_cell + lax.axis_index("cell")
    row_id = lax.broadcasted_iota(jnp.int32, (8, TILE), 0)
    diagonal = lax.broadcasted_iota(jnp.int32, (TILE, TILE), 0) == lax.broadcasted_iota(jnp.int32, (TILE, TILE), 1)
    identity = jnp.where(diagonal, 1.0, 0.0).astype(BF16)

    def one_row(r, carry):
        value = source[r]
        coord_ref[pl.ds(r, 8, stride=rows), :] = value
        centred = jnp.where(row_id < 3, value - 0.5, 0.0)
        length = SCALE * jnp.sum(centred * centred, axis=0, keepdims=True)
        value = jnp.where(row_id == 3, 1.0, jnp.where(row_id == 4, length, centred))
        high, middle, low = split3(value)
        stacked = jnp.concatenate([high, middle, low, high, middle, high], axis=0).astype(BF16)
        turned = lax.dot_general(identity, stacked, BOTH_MINOR, preferred_element_type=F32)
        feature_ref[r] = turned.astype(BF16)
        return carry

    lax.fori_loop(0, rows, one_row, 0, unroll=8)
    tile = coord_ref[3 * rows : 4 * rows, :].T[:8].astype(jnp.int32)
    if masks is not None:
        tile = tile ^ device
        places = [(lax.shift_right_logical(tile, m) & 1) << k for k, m in enumerate(masks)]
        tile = functools.reduce(lambda x, y: x | y, places)
    else:
        tile = tile & (plane - 1)
    place_ref[:, :rows] = tile


def sums_kernel(*refs, rows, start, count, slots, half, first, prepare, before_spans, share):
    last = len(before_spans) > 0
    refs = list(refs)

    def take(n):
        taken = refs[:n]
        del refs[:n]
        return taken

    list_refs, (mix_ref,), feature_refs = take(slots), take(1), take(slots)
    coord_refs, before_refs = (take(slots), take(len(before_spans))) if last else ([], [])
    block_refs = take(prepare)
    tables = [] if prepare else take(2)
    own_ref, peer_ref = take(2) if last else (None, None)
    total_ref = None if last else take(1)[0]
    tables = tables or take(2)
    if last:
        (total_ref,) = take(1)
    centre_ref, coef_ref = tables
    dist_ref, weight_ref = refs
    combos = 2 * half
    plane = centre_ref.shape[0] // 2
    row_id = lax.broadcasted_iota(jnp.int32, (8, TILE), 0)
    blade = lax.axis_index("blade")
    terms = [blade ^ first, blade ^ (first + 1)]

    base = 0
    for block_ref in block_refs:

        def one_tile(p, carry, block_ref=block_ref, base=base):
            value = block_ref[p, 3 * NT : 3 * NT + 8, :]
            centred = jnp.where(row_id < 3, value - 0.5, 0.0)
            length = SCALE * jnp.sum(centred * centred, axis=0, keepdims=True)
            value = jnp.where(row_id == 3, length, jnp.where(row_id == 4, 1.0, (-2.0 * SCALE) * centred))
            high, middle, low = split3(value)
            stacked = jnp.concatenate([high, high, high, middle, middle, low], axis=0)
            centre_ref[base + p] = stacked.astype(BF16)
            mixed = jnp.dot(
                mix_ref[...], block_ref[p, : 3 * NT, :],
                preferred_element_type=F32, precision=lax.Precision.HIGHEST,
            )
            mixed_high = mixed.astype(BF16).astype(F32)
            coef_ref[base + p] = jnp.concatenate([mixed_high, mixed - mixed_high], axis=0).astype(BF16)
            return carry

        lax.fori_loop(0, block_ref.shape[0], one_tile, 0, unroll=4)
        base += block_ref.shape[0]

    units = [(slot, k) for slot in range(slots) for k in range(2)]
    n_units = len(units)
    groups = count // 2

    def unit_of(group, unit):
        slot, k = units[unit]
        r = 2 * group + k
        lists = list_refs[slot]
        return slot, r, lists[terms[0], start + r], lists[terms[1], start + r] + plane

    def distances(group, unit):
        slot, r, a, b = unit_of(group, unit)
        dist_ref[unit] = jnp.dot(
            feature_refs[slot][start + r], jnp.concatenate([centre_ref[a], centre_ref[b]], axis=1),
            preferred_element_type=F32,
        )

    def weights(unit):
        squared = jnp.maximum(dist_ref[unit], 1e-12)
        margin = jnp.maximum(EDGE - squared * lax.rsqrt(squared), 0.0)
        margin_sq = margin * margin
        weight = (margin_sq * margin_sq) * (1.25 * EDGE - margin)
        high = weight.astype(BF16)
        weight_ref[unit, :TILE] = high
        weight_ref[unit, TILE:] = (weight - high.astype(F32)).astype(BF16)

    def contract(group, unit):
        slot, r, a, b = unit_of(group, unit)
        total = lax.dot_general(
            jnp.concatenate([coef_ref[a], coef_ref[b]], axis=1), weight_ref[unit], BOTH_MINOR,
            preferred_element_type=F32,
        )
        total = total[:combos, :TILE] + total[combos:, :TILE] + total[:combos, TILE:]
        for part in range(combos // 8):
            total_ref[slot, pl.ds(r + part * 8 * count, 8, stride=count), :] = total[part * 8 : part * 8 + 8]

    for unit in range(n_units - 1):
        distances(0, unit)

    def one_group(group, carry):
        before = jnp.maximum(group - 1, 0)
        after = jnp.minimum(group + 1, groups - 1)
        for unit in range(n_units):
            if unit < 2:
                contract(before, unit + n_units - 2)
            else:
                contract(group, unit - 2)
            if unit == 0:
                distances(group, n_units - 1)
            else:
                distances(after, unit - 1)
            weights(unit)
        return carry

    lax.fori_loop(0, groups, one_group, 0, unroll=max(n for n in range(1, 11) if groups % n == 0))
    for unit in range(n_units - 2, n_units):
        contract(groups - 1, unit)
    if not last:
        return

    shifts = half // 2
    for slot in range(slots):
        for out, first_row in ((own_ref, 0), (peer_ref, half)):
            for c in range(half):
                for before_ref, (begin, size) in zip(before_refs, before_spans):
                    row = (first_row + c) * count + begin
                    value = total_ref[slot, row : row + size, :]
                    value = value + before_ref[slot, (first_row + c) * size : (first_row + c + 1) * size, :]
                    if c < shifts:
                        row = (c % 3) * rows + start + begin
                        value = value + coord_refs[slot][row : row + size, :]
                    out[slot, c, begin : begin + size] = value


def merge_kernel(own_ref, peer_ref, moved_ref, velocity_ref, *, slots, half):
    shifts = half // 2
    inst = lax.axis_index("inst")
    for which, source in enumerate((own_ref, peer_ref)):
        for slot in range(slots):
            lane = pl.multiple_of((inst ^ which ^ (2 * slot)) * TILE, TILE)
            moved_ref[:, :, pl.ds(lane, TILE)] = source[slot, :shifts]
            velocity_ref[:, :, pl.ds(lane, TILE)] = source[slot, shifts:]


def in_vmem(value):
    return pltpu.with_memory_space_constraint(value, pltpu.VMEM)


def vmem():
    return pl.BlockSpec(memory_space=pltpu.VMEM)


def smem():
    return pl.BlockSpec(memory_space=pltpu.SMEM)


def on_device(cell_coords, centre_points, coefficients, tile_lists, *, sizes):
    n_blade, n_inst, n_cell = sizes["blade"], sizes["inst"], sizes["cell"]
    rows = cell_coords.shape[1]
    terms = tile_lists.shape[2]
    width = centre_points.shape[1]
    slots = n_inst // 2
    half = 2 * 3 * (NT // n_inst)
    block = jnp.concatenate([coefficients, centre_points, jnp.zeros((5, width), F32)], axis=0)
    list_row = jnp.pad(tile_lists[:, 0, :].astype(F32), ((0, 0), (0, TILE - terms)))
    blank = jnp.zeros_like(list_row)
    cell_rows = jnp.stack([cell_coords[0], cell_coords[1], cell_coords[2], list_row] + [blank] * 4, axis=1)

    core = 1
    inner = [("cell", n_cell, b, b) for b in bits_of(n_cell)]
    inner += [("inst", n_inst, b, b * n_cell) for b in bits_of(n_inst) if b != core]
    masks = [mask.bit_length() - 1 for _, _, _, mask in inner] + [(core * n_cell).bit_length() - 1]

    half_plane = block[None]
    for index, (axis, size, bit, _) in enumerate(inner):
        arrived = lax.ppermute(half_plane, axis, flip(size, bit))
        if index == 0:
            arrived, cell_rows = lax.optimization_barrier((arrived, cell_rows))
        half_plane = jnp.concatenate([half_plane, arrived], axis=0)
    others = [lax.ppermute(cell_rows, "inst", flip(n_inst, 2 * s)) for s in range(1, slots)]
    halves = [half_plane]
    for m in range(1, n_blade):
        halves.append(lax.ppermute(half_plane, "blade", flip(n_blade, m)))

    swapped = []
    for m in range(2):
        swapped.append(lax.ppermute(halves[m], "inst", flip(n_inst, core)))
    late = lax.ppermute(jnp.concatenate(halves[2:], axis=0), "inst", flip(n_inst, core))
    swapped += jnp.split(late, n_blade - 2, axis=0)

    if width < TILE:
        device = lax.axis_index("inst") * n_cell + lax.axis_index("cell")
        relative = jnp.arange(n_inst * n_cell) ^ device
        order = sum(((relative >> m) & 1) << k for k, m in enumerate(masks))

        def whole_plane(mine, theirs):
            blocks = jnp.take(jnp.concatenate([mine, theirs], axis=0), order, axis=0)
            blocks = blocks.reshape(-1, TILE // width, 3 * NT + 8, width)
            return [jnp.moveaxis(blocks, 1, 2).reshape(-1, 3 * NT + 8, TILE)]

        plane = n_inst * n_cell * width // TILE
    else:
        def whole_plane(mine, theirs):
            return [mine, theirs]

        plane = n_inst * n_cell
    planes = [whole_plane(*pair) for pair in zip(halves, swapped)]

    params = pltpu.CompilerParams(vmem_limit_bytes=VMEM_LIMIT)

    def cell_prep(cells, *mix):
        out = (
            pltpu.VMEM((rows, TILE, FEATURES), BF16),
            pltpu.VMEM((8 * rows, TILE), F32),
            jax.ShapeDtypeStruct((8, TILE), jnp.int32),
        ) + ((pltpu.VMEM((2 * half, 3 * NT), F32),) if mix else ())
        return pl.pallas_call(
            functools.partial(
                cell_prep_kernel, rows=rows, plane=plane, sizes=sizes, masks=masks if width == TILE else None
            ),
            out_shape=out,
            in_specs=[vmem()] * (1 + len(mix)),
            out_specs=(vmem(),) * len(out),
            compiler_params=params,
            name="cell_prep",
        )(in_vmem(cells), *mix)

    *own_cells, mix = cell_prep(cell_rows, jnp.asarray(spectral_rows(NT, n_inst)))
    prepared = [own_cells]
    prepared += [cell_prep(cells) for cells in others]
    features, coords, places = map(list, zip(*prepared))

    def sums(first, start, count, before=(), before_spans=(), given=(), share=False):
        last = len(before) > 0
        blocks = [] if given else planes[first] + planes[first + 1]
        total = pltpu.VMEM((slots, 2 * half * count, TILE), F32)
        tables = [pltpu.VMEM((2 * plane, n, TILE), BF16) for n in (FEATURES, 4 * half)]
        out = [pltpu.VMEM((slots, half, count, TILE), F32)] * 2 if last else [total]
        scratch = [] if given or share else tables
        operands = [mix, *features, *(coords if last else []), *before, *blocks, *given]
        return pl.pallas_call(
            functools.partial(
                sums_kernel, rows=rows, start=start, count=count, slots=slots, half=half, first=first,
                prepare=len(blocks), before_spans=before_spans, share=share,
            ),
            out_shape=tuple(out + (tables if share else [])),
            in_specs=[smem()] * slots + [vmem()] * len(operands),
            out_specs=(vmem(),) * (len(out) + (2 if share else 0)),
            scratch_shapes=scratch
            + ([total] if last else [])
            + [pltpu.VMEM((2 * slots, TILE, 2 * TILE), F32), pltpu.VMEM((2 * slots, 2 * TILE, 2 * TILE), BF16)],
            compiler_params=params,
        )(*places, *map(in_vmem, operands))

    spans = [(0, rows)] if NEAR_ROWS == 0 else [(0, NEAR_ROWS), (NEAR_ROWS, rows - NEAR_ROWS)]
    before, tables = [], []
    for start, count in spans:
        part, *made = sums(0, start, count, given=tables, share=len(spans) > 1 and not tables)
        before, tables = before + [part], tables or made
    own, peer = sums(2, 0, rows, before=before, before_spans=spans)
    received = lax.ppermute(peer, "inst", flip(n_inst, core))
    out = jax.ShapeDtypeStruct((half // 2, rows, n_inst * TILE), F32)
    moved, velocity = pl.pallas_call(
        functools.partial(merge_kernel, slots=slots, half=half),
        out_shape=(out, out),
        in_specs=[vmem()] * 2,
        out_specs=(vmem(), vmem()),
        compiler_params=params,
        name="merge",
    )(in_vmem(own), in_vmem(received))
    shape = (NT // n_inst, 3, rows, n_inst * TILE)
    return (moved.reshape(shape), velocity.reshape(shape))


def solution(mesh):
    sizes = dict(mesh.shape)
    in_specs = (
        P(None, ("blade", "cell"), "inst"),
        P(None, ("blade", "inst", "cell")),
        P(None, ("blade", "inst", "cell")),
        P(("blade", "cell"), "inst", None),
    )
    out_specs = (P("inst", None, ("blade", "cell"), None), P("inst", None, ("blade", "cell"), None))
    return jax.shard_map(
        functools.partial(on_device, sizes=sizes),
        mesh=mesh, in_specs=in_specs, out_specs=out_specs, check_vma=False,
    )
```

```python
import functools

import jax
import jax.numpy as jnp
import numpy as np
from jax import lax
from jax.experimental import pallas as pl
from jax.experimental.pallas import tpu as pltpu
from jax.sharding import PartitionSpec as P

NT = 8
TILE = 128
RADIUS = 0.4
EDGE = 4.0**0.2
SCALE = (EDGE / RADIUS) ** 2
FEATURES = 48
NEAR_ROWS = 24
VMEM_LIMIT = 16 * 1024 * 1024
BOTH_MINOR = (((1,), (1,)), ((), ()))
F32 = jnp.float32
BF16 = jnp.bfloat16


def spectral_rows(instances, groups):
    later = np.arange(instances)[:, None]
    earlier = np.arange(instances)[None, :]
    distance = (later - earlier).astype(np.float64)
    guarded = np.where(distance == 0, 0.5, np.pi * distance / instances)
    parity = np.where((later - earlier) % 2 == 0, 1.0, -1.0)
    matrix = np.where(distance == 0, 0.0, 0.5 * parity * np.cos(guarded) / np.sin(guarded))
    per = instances // groups
    rows = []
    for group in range(groups):
        own = slice(group * per, (group + 1) * per)
        rows.append(np.concatenate([np.eye(instances)[own], matrix[own]], axis=0))
    return np.stack([np.kron(block, np.eye(3)) for block in rows]).astype(np.float32)


def split3(value):
    high = value.astype(BF16).astype(F32)
    rest = value - high
    middle = rest.astype(BF16).astype(F32)
    return high, middle, rest - middle


def flip(size, bit):
    return [(i, i ^ bit) for i in range(size)]


def bits_of(size):
    return [1 << b for b in range(size.bit_length() - 1)]


def cell_prep_kernel(source, *refs, rows, plane, sizes, masks):
    *refs, staged_ref, sem = refs
    feature_ref, coord_ref, place_ref = refs[-4:-1] if len(refs) == 5 else refs
    if len(refs) == 5:
        mix_ref, mixed_ref = refs[0], refs[-1]
        inst = lax.axis_index("inst")
        mixed_ref[...] = jnp.concatenate([mix_ref[inst], mix_ref[inst ^ 1]], axis=0)
    n_inst, n_cell = sizes["inst"], sizes["cell"]
    device = (lax.axis_index("blade") * n_inst + lax.axis_index("inst")) * n_cell + lax.axis_index("cell")
    row_id = lax.broadcasted_iota(jnp.int32, (8, TILE), 0)
    diagonal = lax.broadcasted_iota(jnp.int32, (TILE, TILE), 0) == lax.broadcasted_iota(jnp.int32, (TILE, TILE), 1)
    identity = jnp.where(diagonal, 1.0, 0.0).astype(BF16)

    tile = source[:, 3, :].T[:8].astype(jnp.int32)
    if masks is not None:
        tile = tile ^ device
        places = [(lax.shift_right_logical(tile, m) & 1) << k for k, m in enumerate(masks)]
        tile = functools.reduce(lambda x, y: x | y, places)
    else:
        tile = tile & (plane - 1)
    staged_ref[:, :rows] = tile
    staged = pltpu.make_async_copy(staged_ref, place_ref, sem)
    staged.start()

    def one_row(r, carry):
        value = source[r]
        coord_ref[pl.ds(r, 8, stride=rows), :] = value
        centred = jnp.where(row_id < 3, value - 0.5, 0.0)
        length = SCALE * jnp.sum(centred * centred, axis=0, keepdims=True)
        value = jnp.where(row_id == 3, 1.0, jnp.where(row_id == 4, length, centred))
        high, middle, low = split3(value)
        stacked = jnp.concatenate([high, middle, low, high, middle, high], axis=0).astype(BF16)
        turned = lax.dot_general(identity, stacked, BOTH_MINOR, preferred_element_type=F32)
        feature_ref[r] = turned.astype(BF16)
        return carry

    lax.fori_loop(0, rows, one_row, 0, unroll=8)
    staged.wait()


def sums_kernel(*refs, rows, start, count, slots, half, first, prepare, before_spans, share):
    last = len(before_spans) > 0
    refs = list(refs)

    def take(n):
        taken = refs[:n]
        del refs[:n]
        return taken

    list_refs, (mix_ref,), feature_refs = take(slots), take(1), take(slots)
    coord_refs, before_refs = (take(slots), take(len(before_spans))) if last else ([], [])
    block_refs = take(prepare)
    tables = [] if prepare else take(2)
    own_ref, peer_ref = take(2) if last else (None, None)
    total_ref = None if last else take(1)[0]
    tables = tables or take(2)
    if last:
        (total_ref,) = take(1)
    centre_ref, coef_ref = tables
    dist_ref, weight_ref = refs
    combos = 2 * half
    plane = centre_ref.shape[0] // 2
    row_id = lax.broadcasted_iota(jnp.int32, (8, TILE), 0)
    blade = lax.axis_index("blade")
    terms = [blade ^ first, blade ^ (first + 1)]

    base = 0
    for block_ref in block_refs:

        def one_tile(p, carry, block_ref=block_ref, base=base):
            value = block_ref[p, 3 * NT : 3 * NT + 8, :]
            centred = jnp.where(row_id < 3, value - 0.5, 0.0)
            length = SCALE * jnp.sum(centred * centred, axis=0, keepdims=True)
            value = jnp.where(row_id == 3, length, jnp.where(row_id == 4, 1.0, (-2.0 * SCALE) * centred))
            high, middle, low = split3(value)
            stacked = jnp.concatenate([high, high, high, middle, middle, low], axis=0)
            centre_ref[base + p] = stacked.astype(BF16)
            mixed = jnp.dot(
                mix_ref[...], block_ref[p, : 3 * NT, :],
                preferred_element_type=F32, precision=lax.Precision.HIGHEST,
            )
            mixed_high = mixed.astype(BF16).astype(F32)
            coef_ref[base + p] = jnp.concatenate([mixed_high, mixed - mixed_high], axis=0).astype(BF16)
            return carry

        lax.fori_loop(0, block_ref.shape[0], one_tile, 0, unroll=4)
        base += block_ref.shape[0]

    units = [(slot, k) for slot in range(slots) for k in range(2)]
    n_units = len(units)
    groups = count // 2

    def unit_of(group, unit):
        slot, k = units[unit]
        r = 2 * group + k
        lists = list_refs[slot]
        return slot, r, lists[terms[0], start + r], lists[terms[1], start + r] + plane

    def distances(group, unit):
        slot, r, a, b = unit_of(group, unit)
        dist_ref[unit] = jnp.dot(
            feature_refs[slot][start + r], jnp.concatenate([centre_ref[a], centre_ref[b]], axis=1),
            preferred_element_type=F32,
        )

    def weights(unit):
        squared = jnp.maximum(dist_ref[unit], 1e-12)
        margin = jnp.maximum(EDGE - squared * lax.rsqrt(squared), 0.0)
        margin_sq = margin * margin
        weight = (margin_sq * margin_sq) * (1.25 * EDGE - margin)
        high = weight.astype(BF16)
        weight_ref[unit, :TILE] = high
        weight_ref[unit, TILE:] = (weight - high.astype(F32)).astype(BF16)

    def contract(group, unit):
        slot, r, a, b = unit_of(group, unit)
        total = lax.dot_general(
            jnp.concatenate([coef_ref[a], coef_ref[b]], axis=1), weight_ref[unit], BOTH_MINOR,
            preferred_element_type=F32,
        )
        total = total[:combos, :TILE] + total[combos:, :TILE] + total[:combos, TILE:]
        for part in range(combos // 8):
            total_ref[slot, pl.ds(r + part * 8 * count, 8, stride=count), :] = total[part * 8 : part * 8 + 8]

    for unit in range(n_units - 1):
        distances(0, unit)

    def one_group(group, carry):
        before = jnp.maximum(group - 1, 0)
        after = jnp.minimum(group + 1, groups - 1)
        for unit in range(n_units):
            if unit < 2:
                contract(before, unit + n_units - 2)
            else:
                contract(group, unit - 2)
            if unit == 0:
                distances(group, n_units - 1)
            else:
                distances(after, unit - 1)
            weights(unit)
        return carry

    lax.fori_loop(0, groups, one_group, 0, unroll=max(n for n in range(1, 11) if groups % n == 0))
    for unit in range(n_units - 2, n_units):
        contract(groups - 1, unit)
    if not last:
        return

    shifts = half // 2
    for slot in range(slots):
        for out, first_row in ((own_ref, 0), (peer_ref, half)):
            for c in range(half):
                for before_ref, (begin, size) in zip(before_refs, before_spans):
                    row = (first_row + c) * count + begin
                    value = total_ref[slot, row : row + size, :]
                    value = value + before_ref[slot, (first_row + c) * size : (first_row + c + 1) * size, :]
                    if c < shifts:
                        row = (c % 3) * rows + start + begin
                        value = value + coord_refs[slot][row : row + size, :]
                    out[slot, c, begin : begin + size] = value


def merge_kernel(own_ref, peer_ref, moved_ref, velocity_ref, *, slots, half):
    shifts = half // 2
    inst = lax.axis_index("inst")
    for which, source in enumerate((own_ref, peer_ref)):
        for slot in range(slots):
            lane = pl.multiple_of((inst ^ which ^ (2 * slot)) * TILE, TILE)
            moved_ref[:, :, pl.ds(lane, TILE)] = source[slot, :shifts]
            velocity_ref[:, :, pl.ds(lane, TILE)] = source[slot, shifts:]


def in_vmem(value):
    return pltpu.with_memory_space_constraint(value, pltpu.VMEM)


def in_smem(value):
    return pltpu.with_memory_space_constraint(value, pltpu.SMEM)


def vmem():
    return pl.BlockSpec(memory_space=pltpu.VMEM)


def smem():
    return pl.BlockSpec(memory_space=pltpu.SMEM)


def on_device(cell_coords, centre_points, coefficients, tile_lists, *, sizes):
    n_blade, n_inst, n_cell = sizes["blade"], sizes["inst"], sizes["cell"]
    rows = cell_coords.shape[1]
    terms = tile_lists.shape[2]
    width = centre_points.shape[1]
    slots = n_inst // 2
    half = 2 * 3 * (NT // n_inst)
    block = jnp.concatenate([coefficients, centre_points, jnp.zeros((5, width), F32)], axis=0)
    list_row = jnp.pad(tile_lists[:, 0, :].astype(F32), ((0, 0), (0, TILE - terms)))
    blank = jnp.zeros_like(list_row)
    cell_rows = jnp.stack([cell_coords[0], cell_coords[1], cell_coords[2], list_row] + [blank] * 4, axis=1)

    core = 1
    inner = [("cell", n_cell, b, b) for b in bits_of(n_cell)]
    inner += [("inst", n_inst, b, b * n_cell) for b in bits_of(n_inst) if b != core]
    masks = [mask.bit_length() - 1 for _, _, _, mask in inner] + [(core * n_cell).bit_length() - 1]

    half_plane = block[None]
    for index, (axis, size, bit, _) in enumerate(inner):
        arrived = lax.ppermute(half_plane, axis, flip(size, bit))
        if index == 0:
            arrived, cell_rows = lax.optimization_barrier((arrived, cell_rows))
        half_plane = jnp.concatenate([half_plane, arrived], axis=0)
    others = [lax.ppermute(cell_rows, "inst", flip(n_inst, 2 * s)) for s in range(1, slots)]
    halves = [half_plane]
    for m in range(1, n_blade):
        halves.append(lax.ppermute(half_plane, "blade", flip(n_blade, m)))

    swapped = []
    for m in range(2):
        swapped.append(lax.ppermute(halves[m], "inst", flip(n_inst, core)))
    late = lax.ppermute(jnp.concatenate(halves[2:], axis=0), "inst", flip(n_inst, core))
    swapped += jnp.split(late, n_blade - 2, axis=0)

    if width < TILE:
        device = lax.axis_index("inst") * n_cell + lax.axis_index("cell")
        relative = jnp.arange(n_inst * n_cell) ^ device
        order = sum(((relative >> m) & 1) << k for k, m in enumerate(masks))

        def whole_plane(mine, theirs):
            blocks = jnp.take(jnp.concatenate([mine, theirs], axis=0), order, axis=0)
            blocks = blocks.reshape(-1, TILE // width, 3 * NT + 8, width)
            return [jnp.moveaxis(blocks, 1, 2).reshape(-1, 3 * NT + 8, TILE)]

        plane = n_inst * n_cell * width // TILE
    else:
        def whole_plane(mine, theirs):
            return [mine, theirs]

        plane = n_inst * n_cell
    planes = [whole_plane(*pair) for pair in zip(halves, swapped)]

    params = pltpu.CompilerParams(vmem_limit_bytes=VMEM_LIMIT)

    def cell_prep(cells, *mix):
        out = (
            pltpu.VMEM((rows, TILE, FEATURES), BF16),
            pltpu.VMEM((8 * rows, TILE), F32),
            pltpu.SMEM((8, TILE), jnp.int32),
        ) + ((pltpu.VMEM((2 * half, 3 * NT), F32),) if mix else ())
        return pl.pallas_call(
            functools.partial(
                cell_prep_kernel, rows=rows, plane=plane, sizes=sizes, masks=masks if width == TILE else None
            ),
            out_shape=out,
            in_specs=[vmem()] * (1 + len(mix)),
            out_specs=(vmem(), vmem(), smem()) + (vmem(),) * len(mix),
            scratch_shapes=[pltpu.VMEM((8, TILE), jnp.int32), pltpu.SemaphoreType.DMA],
            compiler_params=params,
            name="cell_prep",
        )(in_vmem(cells), *mix)

    *own_cells, mix = cell_prep(cell_rows, jnp.asarray(spectral_rows(NT, n_inst)))
    prepared = [own_cells]
    prepared += [cell_prep(cells) for cells in others]
    features, coords, places = map(list, zip(*prepared))

    def sums(first, start, count, before=(), before_spans=(), given=(), share=False):
        last = len(before) > 0
        blocks = [] if given else planes[first] + planes[first + 1]
        total = pltpu.VMEM((slots, 2 * half * count, TILE), F32)
        tables = [pltpu.VMEM((2 * plane, n, TILE), BF16) for n in (FEATURES, 4 * half)]
        out = [pltpu.VMEM((slots, half, count, TILE), F32)] * 2 if last else [total]
        scratch = [] if given or share else tables
        operands = [mix, *features, *(coords if last else []), *before, *blocks, *given]
        return pl.pallas_call(
            functools.partial(
                sums_kernel, rows=rows, start=start, count=count, slots=slots, half=half, first=first,
                prepare=len(blocks), before_spans=before_spans, share=share,
            ),
            out_shape=tuple(out + (tables if share else [])),
            in_specs=[smem()] * slots + [vmem()] * len(operands),
            out_specs=(vmem(),) * (len(out) + (2 if share else 0)),
            scratch_shapes=scratch
            + ([total] if last else [])
            + [pltpu.VMEM((2 * slots, TILE, 2 * TILE), F32), pltpu.VMEM((2 * slots, 2 * TILE, 2 * TILE), BF16)],
            compiler_params=params,
        )(*map(in_smem, places), *map(in_vmem, operands))

    spans = [(0, rows)] if NEAR_ROWS == 0 else [(0, NEAR_ROWS), (NEAR_ROWS, rows - NEAR_ROWS)]
    before, tables = [], []
    for start, count in spans:
        part, *made = sums(0, start, count, given=tables, share=len(spans) > 1 and not tables)
        before, tables = before + [part], tables or made
    own, peer = sums(2, 0, rows, before=before, before_spans=spans)
    received = lax.ppermute(peer, "inst", flip(n_inst, core))
    out = jax.ShapeDtypeStruct((half // 2, rows, n_inst * TILE), F32)
    moved, velocity = pl.pallas_call(
        functools.partial(merge_kernel, slots=slots, half=half),
        out_shape=(out, out),
        in_specs=[vmem()] * 2,
        out_specs=(vmem(), vmem()),
        compiler_params=params,
        name="merge",
    )(in_vmem(own), in_vmem(received))
    shape = (NT // n_inst, 3, rows, n_inst * TILE)
    return (moved.reshape(shape), velocity.reshape(shape))


def solution(mesh):
    sizes = dict(mesh.shape)
    in_specs = (
        P(None, ("blade", "cell"), "inst"),
        P(None, ("blade", "inst", "cell")),
        P(None, ("blade", "inst", "cell")),
        P(("blade", "cell"), "inst", None),
    )
    out_specs = (P("inst", None, ("blade", "cell"), None), P("inst", None, ("blade", "cell"), None))
    return jax.shard_map(
        functools.partial(on_device, sizes=sizes),
        mesh=mesh, in_specs=in_specs, out_specs=out_specs, check_vma=False,
    )
```

```python
import functools

import jax
import jax.numpy as jnp
import numpy as np
from jax import lax
from jax.experimental import pallas as pl
from jax.experimental.pallas import tpu as pltpu
from jax.sharding import PartitionSpec as P

NT = 8
TILE = 128
RADIUS = 0.4
EDGE = 4.0**0.2
SCALE = (EDGE / RADIUS) ** 2
FEATURES = 48
NEAR_ROWS = 24
FAR_ROWS = 0
VMEM_LIMIT = 16 * 1024 * 1024
BOTH_MINOR = (((1,), (1,)), ((), ()))
F32 = jnp.float32
BF16 = jnp.bfloat16


def spectral_rows(instances, groups):
    later = np.arange(instances)[:, None]
    earlier = np.arange(instances)[None, :]
    distance = (later - earlier).astype(np.float64)
    guarded = np.where(distance == 0, 0.5, np.pi * distance / instances)
    parity = np.where((later - earlier) % 2 == 0, 1.0, -1.0)
    matrix = np.where(distance == 0, 0.0, 0.5 * parity * np.cos(guarded) / np.sin(guarded))
    per = instances // groups
    rows = []
    for group in range(groups):
        own = slice(group * per, (group + 1) * per)
        rows.append(np.concatenate([np.eye(instances)[own], matrix[own]], axis=0))
    mix = np.stack([np.kron(block, np.eye(3)) for block in rows]).astype(np.float32)
    parts = []
    for _ in range(3):
        parts.append(mix.astype(jnp.bfloat16).astype(np.float32))
        mix = mix - parts[-1]
    high, middle, low = parts
    return np.concatenate([high, middle, low, high, middle, high], axis=2)


def split3(value):
    high = value.astype(BF16).astype(F32)
    rest = value - high
    middle = rest.astype(BF16).astype(F32)
    return high, middle, rest - middle


def flip(size, bit):
    return [(i, i ^ bit) for i in range(size)]


def bits_of(size):
    return [1 << b for b in range(size.bit_length() - 1)]


def pack_kernel(coef_ref, point_ref, coord_ref, list_ref, mix_ref, block_ref, cell_ref, mixed_ref):
    count = coef_ref.shape[0]
    width = coef_ref.shape[1]
    block_ref[:count] = coef_ref[...]
    block_ref[count:] = jnp.concatenate([point_ref[...], jnp.zeros((5, width), F32)], axis=0)
    size = coord_ref.shape[0]
    cell_ref[:size] = coord_ref[...]
    cell_ref[size:] = jnp.zeros((8, TILE), F32)
    terms, rows = list_ref.shape
    cell_ref[size : size + terms, :rows] = list_ref[...].astype(F32)
    inst = lax.axis_index("inst")
    mixed_ref[...] = jnp.concatenate([mix_ref[inst], mix_ref[inst ^ 1]], axis=0).astype(BF16)


def cell_prep_kernel(cell_ref, feature_ref, place_ref, staged_ref, sem, *, rows, plane, sizes, masks):
    n_inst, n_cell = sizes["inst"], sizes["cell"]
    device = (lax.axis_index("blade") * n_inst + lax.axis_index("inst")) * n_cell + lax.axis_index("cell")
    row_id = lax.broadcasted_iota(jnp.int32, (8, TILE), 0)
    diagonal = lax.broadcasted_iota(jnp.int32, (TILE, TILE), 0) == lax.broadcasted_iota(jnp.int32, (TILE, TILE), 1)
    identity = jnp.where(diagonal, 1.0, 0.0).astype(BF16)

    tile = cell_ref[3 * rows :, :].astype(jnp.int32)
    if masks is not None:
        tile = tile ^ device
        places = [(lax.shift_right_logical(tile, m) & 1) << k for k, m in enumerate(masks)]
        tile = functools.reduce(lambda x, y: x | y, places)
    else:
        tile = tile & (plane - 1)
    staged_ref[...] = tile
    staged = pltpu.make_async_copy(staged_ref, place_ref, sem)
    staged.start()

    def one_row(r, carry):
        value = jnp.concatenate([cell_ref[pl.ds(r, 3, stride=rows), :], jnp.zeros((5, TILE), F32)], axis=0)
        centred = jnp.where(row_id < 3, value - 0.5, 0.0)
        length = SCALE * jnp.sum(centred * centred, axis=0, keepdims=True)
        value = jnp.where(row_id == 3, 1.0, jnp.where(row_id == 4, length, centred))
        high, middle, low = split3(value)
        stacked = jnp.concatenate([high, middle, low, high, middle, high], axis=0).astype(BF16)
        turned = lax.dot_general(identity, stacked, BOTH_MINOR, preferred_element_type=F32)
        feature_ref[r] = turned.astype(BF16)
        return carry

    lax.fori_loop(0, rows, one_row, 0, unroll=8)
    staged.wait()


def sums_kernel(*refs, rows, start, count, slots, half, first, prepare, before_spans, share):
    last = len(before_spans) > 0
    refs = list(refs)

    def take(n):
        taken = refs[:n]
        del refs[:n]
        return taken

    list_refs, (mix_ref,), feature_refs = take(slots), take(1), take(slots)
    coord_refs, before_refs = (take(slots), take(len(before_spans))) if last else ([], [])
    block_refs = take(prepare)
    tables = [] if prepare else take(2)
    own_ref, peer_ref = take(2) if last else (None, None)
    total_ref = None if last else take(1)[0]
    tables = tables or take(2)
    if last:
        (total_ref,) = take(1)
    centre_ref, coef_ref = tables
    dist_ref, weight_ref = refs
    combos = 2 * half
    plane = centre_ref.shape[0] // 2
    row_id = lax.broadcasted_iota(jnp.int32, (8, TILE), 0)
    blade = lax.axis_index("blade")
    terms = [blade ^ first, blade ^ (first + 1)]

    base = 0
    for block_ref in block_refs:

        def one_tile(p, carry, block_ref=block_ref, base=base):
            value = block_ref[p, 3 * NT : 3 * NT + 8, :]
            centred = jnp.where(row_id < 3, value - 0.5, 0.0)
            length = SCALE * jnp.sum(centred * centred, axis=0, keepdims=True)
            value = jnp.where(row_id == 3, length, jnp.where(row_id == 4, 1.0, (-2.0 * SCALE) * centred))
            high, middle, low = split3(value)
            stacked = jnp.concatenate([high, high, high, middle, middle, low], axis=0)
            centre_ref[base + p] = stacked.astype(BF16)
            high, middle, low = split3(block_ref[p, : 3 * NT, :])
            stacked = jnp.concatenate([high, high, high, middle, middle, low], axis=0).astype(BF16)
            mixed = jnp.dot(mix_ref[...], stacked, preferred_element_type=F32)
            mixed_high = mixed.astype(BF16).astype(F32)
            coef_ref[base + p] = jnp.concatenate([mixed_high, mixed - mixed_high], axis=0).astype(BF16)
            return carry

        lax.fori_loop(0, block_ref.shape[0], one_tile, 0, unroll=4)
        base += block_ref.shape[0]

    units = [(slot, k) for slot in range(slots) for k in range(2)]
    n_units = len(units)
    groups = count // 2

    def unit_of(group, unit):
        slot, k = units[unit]
        r = 2 * group + k
        lists = list_refs[slot]
        return slot, r, lists[terms[0], start + r], lists[terms[1], start + r] + plane

    def distances(group, unit):
        slot, r, a, b = unit_of(group, unit)
        dist_ref[unit] = jnp.dot(
            feature_refs[slot][start + r], jnp.concatenate([centre_ref[a], centre_ref[b]], axis=1),
            preferred_element_type=F32,
        )

    def weights(unit):
        squared = jnp.clip(dist_ref[unit], 1e-12, EDGE * EDGE)
        margin = EDGE - squared * lax.rsqrt(squared)
        margin_sq = margin * margin
        weight = (margin_sq * margin_sq) * (1.25 * EDGE - margin)
        high = weight.astype(BF16)
        weight_ref[unit, :TILE] = high
        weight_ref[unit, TILE:] = (weight - high.astype(F32)).astype(BF16)

    def contract(group, unit):
        slot, r, a, b = unit_of(group, unit)
        total = lax.dot_general(
            jnp.concatenate([coef_ref[a], coef_ref[b]], axis=1), weight_ref[unit], BOTH_MINOR,
            preferred_element_type=F32,
        )
        total = total[:combos, :TILE] + total[combos:, :TILE] + total[:combos, TILE:]
        for part in range(combos // 8):
            total_ref[slot, pl.ds(r + part * 8 * count, 8, stride=count), :] = total[part * 8 : part * 8 + 8]

    for unit in range(n_units - 1):
        distances(0, unit)

    def one_group(group, carry):
        before = jnp.maximum(group - 1, 0)
        after = jnp.minimum(group + 1, groups - 1)
        for unit in range(n_units):
            if unit < 2:
                contract(before, unit + n_units - 2)
            else:
                contract(group, unit - 2)
            if unit == 0:
                distances(group, n_units - 1)
            else:
                distances(after, unit - 1)
            weights(unit)
        return carry

    lax.fori_loop(0, groups, one_group, 0, unroll=max(n for n in range(1, 11) if groups % n == 0))
    for unit in range(n_units - 2, n_units):
        contract(groups - 1, unit)
    if not last:
        return

    shifts = half // 2
    for slot in range(slots):
        for out, first_row in ((own_ref, 0), (peer_ref, half)):
            for c in range(half):
                for before_ref, (begin, size) in zip(before_refs, before_spans):
                    row = (first_row + c) * count + begin
                    value = total_ref[slot, row : row + size, :]
                    value = value + before_ref[slot, (first_row + c) * size : (first_row + c + 1) * size, :]
                    if c < shifts:
                        row = (c % 3) * rows + start + begin
                        value = value + coord_refs[slot][row : row + size, :]
                    out[slot, c, begin : begin + size] = value


def merge_kernel(own_ref, peer_ref, *refs, slots, half, start, count):
    shifts = half // 2
    moved_ref, velocity_ref, stage_ref, sems = refs[-4:]
    inst = lax.axis_index("inst")
    copies = []
    for c in range(half):
        for which, source in enumerate((own_ref, peer_ref)):
            for slot in range(slots):
                lane = pl.multiple_of((inst ^ which ^ (2 * slot)) * TILE, TILE)
                stage_ref[c, :, pl.ds(lane, TILE)] = source[slot, c]
        out = moved_ref if c < shifts else velocity_ref
        copy = pltpu.make_async_copy(stage_ref.at[c], out.at[c % shifts, pl.ds(start, count)], sems.at[c])
        copy.start()
        copies.append(copy)
    for copy in copies:
        copy.wait()


def in_vmem(value):
    return pltpu.with_memory_space_constraint(value, pltpu.VMEM)


def in_smem(value):
    return pltpu.with_memory_space_constraint(value, pltpu.SMEM)


def in_hbm(value):
    return pltpu.with_memory_space_constraint(value, pltpu.HBM)


def vmem():
    return pl.BlockSpec(memory_space=pltpu.VMEM)


def hbm():
    return pl.BlockSpec(memory_space=pl.ANY)


def smem():
    return pl.BlockSpec(memory_space=pltpu.SMEM)


def on_device(cell_coords, centre_points, coefficients, tile_lists, *, sizes):
    n_blade, n_inst, n_cell = sizes["blade"], sizes["inst"], sizes["cell"]
    rows = cell_coords.shape[1]
    width = centre_points.shape[1]
    slots = n_inst // 2
    half = 2 * 3 * (NT // n_inst)
    params = pltpu.CompilerParams(vmem_limit_bytes=VMEM_LIMIT)
    given = (
        coefficients, centre_points, cell_coords.reshape(3 * rows, TILE), tile_lists[:, 0, :].T,
        jnp.asarray(spectral_rows(NT, n_inst)),
    )
    block, cells, mix = pl.pallas_call(
        pack_kernel,
        out_shape=(
            pltpu.VMEM((3 * NT + 8, width), F32),
            pltpu.VMEM((3 * rows + 8, TILE), F32),
            pltpu.VMEM((2 * half, 18 * NT), BF16),
        ),
        in_specs=[vmem()] * len(given),
        out_specs=(vmem(),) * 3,
        compiler_params=params,
        name="pack",
    )(*map(in_hbm, given))
    core = 1
    inner = [("cell", n_cell, b, b) for b in bits_of(n_cell)]
    inner += [("inst", n_inst, b, b * n_cell) for b in bits_of(n_inst) if b != core]
    masks = [mask.bit_length() - 1 for _, _, _, mask in inner] + [(core * n_cell).bit_length() - 1]

    plane = n_inst * n_cell * width // TILE

    def cell_prep(cells):
        return pl.pallas_call(
            functools.partial(
                cell_prep_kernel, rows=rows, plane=plane, sizes=sizes, masks=masks if width == TILE else None
            ),
            out_shape=(pltpu.VMEM((rows, TILE, FEATURES), BF16), pltpu.SMEM((8, TILE), jnp.int32)),
            in_specs=[vmem()],
            out_specs=(vmem(), smem()),
            scratch_shapes=[pltpu.VMEM((8, TILE), jnp.int32), pltpu.SemaphoreType.DMA],
            compiler_params=params,
            name="cell_prep",
        )(in_vmem(cells))

    half_plane = block[None]
    joint = inner[-2:]
    for axis, size, bit, _ in inner[:-2]:
        half_plane = jnp.concatenate([half_plane, lax.ppermute(half_plane, axis, flip(size, bit))], axis=0)
    pieces = [half_plane]
    for combination in range(1, 1 << len(joint)):
        mask = sum(joint[k][3] for k in range(len(joint)) if combination >> k & 1)
        pieces.append(lax.ppermute(half_plane, ("inst", "cell"), flip(n_inst * n_cell, mask)))
    half_plane = jnp.concatenate(pieces, axis=0)
    others = [lax.ppermute(cells, "inst", flip(n_inst, 2 * k)) for k in range(1, slots)]
    prepared = [cell_prep(cells)]
    halves = [half_plane]
    for m in range(1, n_blade):
        halves.append(lax.ppermute(half_plane, "blade", flip(n_blade, m)))

    swapped = []
    for m in range(2):
        swapped.append(lax.ppermute(halves[m], "inst", flip(n_inst, core)))
    late = lax.ppermute(jnp.concatenate(halves[2:], axis=0), "inst", flip(n_inst, core))
    swapped += jnp.split(late, n_blade - 2, axis=0)

    if width < TILE:
        device = lax.axis_index("inst") * n_cell + lax.axis_index("cell")
        relative = jnp.arange(n_inst * n_cell) ^ device
        order = sum(((relative >> m) & 1) << k for k, m in enumerate(masks))

        def whole_plane(mine, theirs):
            blocks = jnp.take(jnp.concatenate([mine, theirs], axis=0), order, axis=0)
            blocks = blocks.reshape(-1, TILE // width, 3 * NT + 8, width)
            return [jnp.moveaxis(blocks, 1, 2).reshape(-1, 3 * NT + 8, TILE)]

    else:
        def whole_plane(mine, theirs):
            return [mine, theirs]

    planes = [whole_plane(*pair) for pair in zip(halves, swapped)]

    prepared += [cell_prep(other) for other in others]
    features, places = map(list, zip(*prepared))
    coords = [cells] + others

    def sums(first, start, count, before=(), before_spans=(), given=(), share=False):
        last = len(before) > 0
        blocks = [] if given else planes[first] + planes[first + 1]
        total = pltpu.VMEM((slots, 2 * half * count, TILE), F32)
        tables = [pltpu.VMEM((2 * plane, n, TILE), BF16) for n in (FEATURES, 4 * half)]
        out = [pltpu.VMEM((slots, half, count, TILE), F32)] * 2 if last else [total]
        scratch = [] if given or share else tables
        operands = [mix, *features, *(coords if last else []), *before, *blocks, *given]
        return pl.pallas_call(
            functools.partial(
                sums_kernel, rows=rows, start=start, count=count, slots=slots, half=half, first=first,
                prepare=len(blocks), before_spans=before_spans, share=share,
            ),
            out_shape=tuple(out + (tables if share else [])),
            in_specs=[smem()] * slots + [vmem()] * len(operands),
            out_specs=(vmem(),) * (len(out) + (2 if share else 0)),
            scratch_shapes=scratch
            + ([total] if last else [])
            + [pltpu.VMEM((2 * slots, TILE, 2 * TILE), F32), pltpu.VMEM((2 * slots, 2 * TILE, 2 * TILE), BF16)],
            compiler_params=params,
        )(*map(in_smem, places), *map(in_vmem, operands))

    def spans_of(lead):
        return [(0, lead), (lead, rows - lead)] if lead else [(0, rows)]

    spans = spans_of(NEAR_ROWS)
    before, tables = [], []
    for start, count in spans:
        part, *made = sums(0, start, count, given=tables, share=len(spans) > 1 and not tables)
        before, tables = before + [part], tables or made
    pieces, tables = [], []
    if FAR_ROWS:
        spans = spans_of(FAR_ROWS)
        parts = [([part], [(0, count)]) for part, (_, count) in zip(before, spans)]
    else:
        parts, spans = [(before, spans)], [(0, rows)]
    for (part, part_spans), (start, count) in zip(parts, spans):
        own, peer, *made = sums(
            2, start, count, before=part, before_spans=part_spans,
            given=tables, share=len(spans) > 1 and not tables,
        )
        tables = tables or made
        pieces.append((own, lax.ppermute(peer, "inst", flip(n_inst, core))))
    out = jax.ShapeDtypeStruct((half // 2, rows, n_inst * TILE), F32)
    outputs = ()
    for (start, count), piece in zip(spans, pieces):
        outputs = pl.pallas_call(
            functools.partial(merge_kernel, slots=slots, half=half, start=start, count=count),
            out_shape=(out, out),
            in_specs=[vmem()] * 2 + [hbm()] * len(outputs),
            out_specs=(hbm(), hbm()),
            input_output_aliases={2 + i: i for i in range(len(outputs))},
            scratch_shapes=[
                pltpu.VMEM((half, count, n_inst * TILE), F32), pltpu.SemaphoreType.DMA((half,)),
            ],
            compiler_params=params,
        )(*map(in_vmem, piece), *outputs)
    moved, velocity = outputs
    shape = (NT // n_inst, 3, rows, n_inst * TILE)
    return (moved.reshape(shape), velocity.reshape(shape))


def solution(mesh):
    sizes = dict(mesh.shape)
    in_specs = (
        P(None, ("blade", "cell"), "inst"),
        P(None, ("blade", "inst", "cell")),
        P(None, ("blade", "inst", "cell")),
        P(("blade", "cell"), "inst", None),
    )
    out_specs = (P("inst", None, ("blade", "cell"), None), P("inst", None, ("blade", "cell"), None))
    return jax.shard_map(
        functools.partial(on_device, sizes=sizes),
        mesh=mesh, in_specs=in_specs, out_specs=out_specs, check_vma=False,
    )
```

```python
import functools

import jax
import jax.numpy as jnp
import numpy as np
from jax import lax
from jax.experimental import pallas as pl
from jax.experimental.pallas import tpu as pltpu
from jax.sharding import PartitionSpec as P

NT = 8
TILE = 128
RADIUS = 0.4
EDGE = 4.0**0.2
SCALE = (EDGE / RADIUS) ** 2
FEATURES = 48
VMEM_LIMIT = 16 * 1024 * 1024
BOTH_MINOR = (((1,), (1,)), ((), ()))
F32 = jnp.float32
BF16 = jnp.bfloat16


def spectral_rows(instances, groups):
    later = np.arange(instances)[:, None]
    earlier = np.arange(instances)[None, :]
    distance = (later - earlier).astype(np.float64)
    guarded = np.where(distance == 0, 0.5, np.pi * distance / instances)
    parity = np.where((later - earlier) % 2 == 0, 1.0, -1.0)
    matrix = np.where(distance == 0, 0.0, 0.5 * parity * np.cos(guarded) / np.sin(guarded))
    per = instances // groups
    rows = []
    for group in range(groups):
        own = slice(group * per, (group + 1) * per)
        rows.append(np.concatenate([np.eye(instances)[own], matrix[own]], axis=0))
    mix = np.stack([np.kron(block, np.eye(3)) for block in rows]).astype(np.float32)
    parts = []
    for _ in range(3):
        parts.append(mix.astype(jnp.bfloat16).astype(np.float32))
        mix = mix - parts[-1]
    high, middle, low = parts
    return np.concatenate([high, middle, low, high, middle, high], axis=2)


def split3(value):
    high = value.astype(BF16).astype(F32)
    rest = value - high
    middle = rest.astype(BF16).astype(F32)
    return high, middle, rest - middle


def flip(size, bit):
    return [(i, i ^ bit) for i in range(size)]


def bits_of(size):
    return [1 << b for b in range(size.bit_length() - 1)]


def pack_kernel(coef_ref, point_ref, coord_ref, list_ref, mix_ref, block_ref, cell_ref, mixed_ref):
    count = coef_ref.shape[0]
    width = coef_ref.shape[1]
    block_ref[:count] = coef_ref[...]
    block_ref[count:] = jnp.concatenate([point_ref[...], jnp.zeros((5, width), F32)], axis=0)
    size = coord_ref.shape[0]
    cell_ref[:size] = coord_ref[...]
    cell_ref[size:] = jnp.zeros((8, TILE), F32)
    terms, rows = list_ref.shape
    cell_ref[size : size + terms, :rows] = list_ref[...].astype(F32)
    inst = lax.axis_index("inst")
    mixed_ref[...] = jnp.concatenate([mix_ref[inst], mix_ref[inst ^ 1]], axis=0).astype(BF16)


def cell_prep_kernel(cell_ref, feature_ref, place_ref, staged_ref, sem, *, rows, plane, sizes, masks):
    n_inst, n_cell = sizes["inst"], sizes["cell"]
    device = (lax.axis_index("blade") * n_inst + lax.axis_index("inst")) * n_cell + lax.axis_index("cell")
    row_id = lax.broadcasted_iota(jnp.int32, (8, TILE), 0)
    diagonal = lax.broadcasted_iota(jnp.int32, (TILE, TILE), 0) == lax.broadcasted_iota(jnp.int32, (TILE, TILE), 1)
    identity = jnp.where(diagonal, 1.0, 0.0).astype(BF16)

    tile = cell_ref[3 * rows :, :].astype(jnp.int32)
    if masks is not None:
        tile = tile ^ device
        places = [(lax.shift_right_logical(tile, m) & 1) << k for k, m in enumerate(masks)]
        tile = functools.reduce(lambda x, y: x | y, places)
    else:
        tile = tile & (plane - 1)
    staged_ref[...] = tile
    staged = pltpu.make_async_copy(staged_ref, place_ref, sem)
    staged.start()

    def one_row(r, carry):
        value = jnp.concatenate([cell_ref[pl.ds(r, 3, stride=rows), :], jnp.zeros((5, TILE), F32)], axis=0)
        centred = jnp.where(row_id < 3, value - 0.5, 0.0)
        length = SCALE * jnp.sum(centred * centred, axis=0, keepdims=True)
        value = jnp.where(row_id == 3, 1.0, jnp.where(row_id == 4, length, centred))
        high, middle, low = split3(value)
        stacked = jnp.concatenate([high, middle, low, high, middle, high], axis=0).astype(BF16)
        turned = lax.dot_general(identity, stacked, BOTH_MINOR, preferred_element_type=F32)
        feature_ref[r] = turned.astype(BF16)
        return carry

    lax.fori_loop(0, rows, one_row, 0, unroll=20)
    staged.wait()


def sums_kernel(*refs, rows, start, count, slots, half, first, prepare, before_spans, share):
    last = len(before_spans) > 0
    refs = list(refs)

    def take(n):
        taken = refs[:n]
        del refs[:n]
        return taken

    list_refs, (mix_ref,), feature_refs = take(slots), take(1), take(slots)
    coord_refs, before_refs = (take(slots), take(len(before_spans))) if last else ([], [])
    block_refs = take(prepare)
    tables = [] if prepare else take(2)
    own_ref, peer_ref = take(2) if last else (None, None)
    total_ref = None if last else take(1)[0]
    tables = tables or take(2)
    if last:
        (total_ref,) = take(1)
    centre_ref, coef_ref = tables
    dist_ref, weight_ref = refs
    combos = 2 * half
    plane = centre_ref.shape[0] // 2
    row_id = lax.broadcasted_iota(jnp.int32, (8, TILE), 0)
    blade = lax.axis_index("blade")
    terms = [blade ^ first, blade ^ (first + 1)]

    base = 0
    for block_ref in block_refs:

        def one_tile(p, carry, block_ref=block_ref, base=base):
            value = block_ref[p, 3 * NT : 3 * NT + 8, :]
            centred = jnp.where(row_id < 3, value - 0.5, 0.0)
            length = SCALE * jnp.sum(centred * centred, axis=0, keepdims=True)
            value = jnp.where(row_id == 3, length, jnp.where(row_id == 4, 1.0, (-2.0 * SCALE) * centred))
            high, middle, low = split3(value)
            stacked = jnp.concatenate([high, high, high, middle, middle, low], axis=0)
            centre_ref[base + p] = stacked.astype(BF16)
            high, middle, low = split3(block_ref[p, : 3 * NT, :])
            stacked = jnp.concatenate([high, high, high, middle, middle, low], axis=0).astype(BF16)
            mixed = jnp.dot(mix_ref[...], stacked, preferred_element_type=F32)
            mixed_high = mixed.astype(BF16).astype(F32)
            coef_ref[base + p] = jnp.concatenate([mixed_high, mixed - mixed_high], axis=0).astype(BF16)
            return carry

        lax.fori_loop(0, block_ref.shape[0], one_tile, 0, unroll=4)
        base += block_ref.shape[0]

    units = [(slot, k) for slot in range(slots) for k in range(2)]
    n_units = len(units)
    groups = count // 2

    def unit_of(group, unit):
        slot, k = units[unit]
        r = 2 * group + k
        lists = list_refs[slot]
        return slot, r, lists[terms[0], start + r], lists[terms[1], start + r] + plane

    def distances(group, unit):
        slot, r, a, b = unit_of(group, unit)
        dist_ref[unit] = jnp.dot(
            feature_refs[slot][start + r], jnp.concatenate([centre_ref[a], centre_ref[b]], axis=1),
            preferred_element_type=F32,
        )

    def weights(unit):
        squared = jnp.clip(dist_ref[unit], 1e-12, EDGE * EDGE)
        margin = EDGE - squared * lax.rsqrt(squared)
        margin_sq = margin * margin
        weight = (margin_sq * margin_sq) * (1.25 * EDGE - margin)
        high = weight.astype(BF16)
        weight_ref[unit, :TILE] = high
        weight_ref[unit, TILE:] = (weight - high.astype(F32)).astype(BF16)

    def contract(group, unit):
        slot, r, a, b = unit_of(group, unit)
        total = lax.dot_general(
            jnp.concatenate([coef_ref[a], coef_ref[b]], axis=1), weight_ref[unit], BOTH_MINOR,
            preferred_element_type=F32,
        )
        total = total[:combos, :TILE] + total[combos:, :TILE] + total[:combos, TILE:]
        for part in range(combos // 8):
            total_ref[slot, pl.ds(r + part * 8 * count, 8, stride=count), :] = total[part * 8 : part * 8 + 8]

    for unit in range(n_units - 1):
        distances(0, unit)

    def one_group(group, carry):
        before = jnp.maximum(group - 1, 0)
        after = jnp.minimum(group + 1, groups - 1)
        for unit in range(n_units):
            if unit < 2:
                contract(before, unit + n_units - 2)
            else:
                contract(group, unit - 2)
            if unit == 0:
                distances(group, n_units - 1)
            else:
                distances(after, unit - 1)
            weights(unit)
        return carry

    lax.fori_loop(0, groups, one_group, 0, unroll=max(n for n in range(1, 11) if groups % n == 0))
    for unit in range(n_units - 2, n_units):
        contract(groups - 1, unit)
    if not last:
        return

    shifts = half // 2
    for slot in range(slots):
        for out, first_row in ((own_ref, 0), (peer_ref, half)):
            for c in range(half):
                for before_ref, (begin, size) in zip(before_refs, before_spans):
                    row = (first_row + c) * count + begin
                    value = total_ref[slot, row : row + size, :]
                    value = value + before_ref[slot, (first_row + c) * size : (first_row + c + 1) * size, :]
                    if c < shifts:
                        row = (c % 3) * rows + start + begin
                        value = value + coord_refs[slot][row : row + size, :]
                    out[slot, c, begin : begin + size] = value


def place_kernel(source_ref, *refs, slots, half, which):
    moved_ref, velocity_ref, sems = refs[-3:]
    shifts = half // 2
    inst = lax.axis_index("inst")
    copies = []
    for slot in range(slots):
        lane = pl.multiple_of((inst ^ which ^ (2 * slot)) * TILE, TILE)
        for part, out in enumerate((moved_ref, velocity_ref)):
            copy = pltpu.make_async_copy(
                source_ref.at[slot, pl.ds(part * shifts, shifts)], out.at[:, :, pl.ds(lane, TILE)],
                sems.at[2 * slot + part],
            )
            copy.start()
            copies.append(copy)
    for copy in copies:
        copy.wait()


def in_vmem(value):
    return pltpu.with_memory_space_constraint(value, pltpu.VMEM)


def in_smem(value):
    return pltpu.with_memory_space_constraint(value, pltpu.SMEM)


def in_hbm(value):
    return pltpu.with_memory_space_constraint(value, pltpu.HBM)


def vmem():
    return pl.BlockSpec(memory_space=pltpu.VMEM)


def hbm():
    return pl.BlockSpec(memory_space=pl.ANY)


def smem():
    return pl.BlockSpec(memory_space=pltpu.SMEM)


def on_device(cell_coords, centre_points, coefficients, tile_lists, *, sizes):
    n_blade, n_inst, n_cell = sizes["blade"], sizes["inst"], sizes["cell"]
    rows = cell_coords.shape[1]
    width = centre_points.shape[1]
    slots = n_inst // 2
    half = 2 * 3 * (NT // n_inst)
    params = pltpu.CompilerParams(vmem_limit_bytes=VMEM_LIMIT)
    given = (
        coefficients, centre_points, cell_coords.reshape(3 * rows, TILE), tile_lists[:, 0, :].T,
        jnp.asarray(spectral_rows(NT, n_inst)),
    )
    block, cells, mix = pl.pallas_call(
        pack_kernel,
        out_shape=(
            pltpu.VMEM((3 * NT + 8, width), F32),
            pltpu.VMEM((3 * rows + 8, TILE), F32),
            pltpu.VMEM((2 * half, 18 * NT), BF16),
        ),
        in_specs=[vmem()] * len(given),
        out_specs=(vmem(),) * 3,
        compiler_params=params,
        name="pack",
    )(*map(in_hbm, given))
    core = 1
    inner = [("cell", n_cell, b, b) for b in bits_of(n_cell)]
    inner += [("inst", n_inst, b, b * n_cell) for b in bits_of(n_inst) if b != core]
    masks = [mask.bit_length() - 1 for _, _, _, mask in inner] + [(core * n_cell).bit_length() - 1]

    plane = n_inst * n_cell * width // TILE

    def cell_prep(cells):
        return pl.pallas_call(
            functools.partial(
                cell_prep_kernel, rows=rows, plane=plane, sizes=sizes, masks=masks if width == TILE else None
            ),
            out_shape=(pltpu.VMEM((rows, TILE, FEATURES), BF16), pltpu.SMEM((8, TILE), jnp.int32)),
            in_specs=[vmem()],
            out_specs=(vmem(), smem()),
            scratch_shapes=[pltpu.VMEM((8, TILE), jnp.int32), pltpu.SemaphoreType.DMA],
            compiler_params=params,
            name="cell_prep",
        )(in_vmem(cells))

    half_plane = block[None]
    joint = inner[-2:]
    for axis, size, bit, _ in inner[:-2]:
        half_plane = jnp.concatenate([half_plane, lax.ppermute(half_plane, axis, flip(size, bit))], axis=0)
    pieces = [half_plane]
    for combination in range(1, 1 << len(joint)):
        mask = sum(joint[k][3] for k in range(len(joint)) if combination >> k & 1)
        pieces.append(lax.ppermute(half_plane, ("inst", "cell"), flip(n_inst * n_cell, mask)))
    half_plane = jnp.concatenate(pieces, axis=0)
    others = [lax.ppermute(cells, "inst", flip(n_inst, 2 * k)) for k in range(1, slots)]
    prepared = [cell_prep(cells)]
    halves = [half_plane]
    for m in range(1, n_blade):
        halves.append(lax.ppermute(half_plane, "blade", flip(n_blade, m)))

    swapped = []
    for m in range(2):
        swapped.append(lax.ppermute(halves[m], "inst", flip(n_inst, core)))
    late = lax.ppermute(jnp.concatenate(halves[2:], axis=0), "inst", flip(n_inst, core))
    swapped += jnp.split(late, n_blade - 2, axis=0)

    if width < TILE:
        device = lax.axis_index("inst") * n_cell + lax.axis_index("cell")
        relative = jnp.arange(n_inst * n_cell) ^ device
        order = sum(((relative >> m) & 1) << k for k, m in enumerate(masks))

        def whole_plane(mine, theirs):
            blocks = jnp.take(jnp.concatenate([mine, theirs], axis=0), order, axis=0)
            blocks = blocks.reshape(-1, TILE // width, 3 * NT + 8, width)
            return [jnp.moveaxis(blocks, 1, 2).reshape(-1, 3 * NT + 8, TILE)]

    else:
        def whole_plane(mine, theirs):
            return [mine, theirs]

    planes = [whole_plane(*pair) for pair in zip(halves, swapped)]

    prepared += [cell_prep(other) for other in others]
    features, places = map(list, zip(*prepared))
    coords = [cells] + others

    def sums(first, start, count, before=(), before_spans=(), given=(), share=False):
        last = len(before) > 0
        blocks = [] if given else planes[first] + planes[first + 1]
        total = pltpu.VMEM((slots, 2 * half * count, TILE), F32)
        tables = [pltpu.VMEM((2 * plane, n, TILE), BF16) for n in (FEATURES, 4 * half)]
        out = [pltpu.VMEM((slots, half, count, TILE), F32)] * 2 if last else [total]
        scratch = [] if given or share else tables
        operands = [mix, *features, *(coords if last else []), *before, *blocks, *given]
        return pl.pallas_call(
            functools.partial(
                sums_kernel, rows=rows, start=start, count=count, slots=slots, half=half, first=first,
                prepare=len(blocks), before_spans=before_spans, share=share,
            ),
            out_shape=tuple(out + (tables if share else [])),
            in_specs=[smem()] * slots + [vmem()] * len(operands),
            out_specs=(vmem(),) * (len(out) + (2 if share else 0)),
            scratch_shapes=scratch
            + ([total] if last else [])
            + [pltpu.VMEM((2 * slots, TILE, 2 * TILE), F32), pltpu.VMEM((2 * slots, 2 * TILE, 2 * TILE), BF16)],
            compiler_params=params,
        )(*map(in_smem, places), *map(in_vmem, operands))

    lead = rows * 3 // 5 // 8 * 8
    spans = [(0, lead), (lead, rows - lead)] if lead else [(0, rows)]
    before, tables = [], []
    for start, count in spans:
        part, *made = sums(0, start, count, given=tables, share=len(spans) > 1 and not tables)
        before, tables = before + [part], tables or made
    own, peer = sums(2, 0, rows, before=before, before_spans=spans)
    received = lax.ppermute(peer, "inst", flip(n_inst, core))
    out = jax.ShapeDtypeStruct((half // 2, rows, n_inst * TILE), F32)
    outputs = ()
    for index, source in enumerate((own, received)):
        outputs = pl.pallas_call(
            functools.partial(place_kernel, slots=slots, half=half, which=index),
            out_shape=(out, out),
            in_specs=[vmem()] + [hbm()] * len(outputs),
            out_specs=(hbm(), hbm()),
            input_output_aliases={1 + i: i for i in range(len(outputs))},
            scratch_shapes=[pltpu.SemaphoreType.DMA((2 * slots,))],
            compiler_params=params,
        )(in_vmem(source), *outputs)
    moved, velocity = outputs
    shape = (NT // n_inst, 3, rows, n_inst * TILE)
    return (moved.reshape(shape), velocity.reshape(shape))


def solution(mesh):
    sizes = dict(mesh.shape)
    in_specs = (
        P(None, ("blade", "cell"), "inst"),
        P(None, ("blade", "inst", "cell")),
        P(None, ("blade", "inst", "cell")),
        P(("blade", "cell"), "inst", None),
    )
    out_specs = (P("inst", None, ("blade", "cell"), None), P("inst", None, ("blade", "cell"), None))
    return jax.shard_map(
        functools.partial(on_device, sizes=sizes),
        mesh=mesh, in_specs=in_specs, out_specs=out_specs, check_vma=False,
    )
```
